32 devices in a mesh: groups: 2 (over y), seq: 4 (over z), head: 2 (over x), rep: 2 (over core).
Axes of the slice: x: 2, y: 2, z: 4, core: 2. Of those that a mesh axis runs over, the one named last changes fastest.
Arguments:
- queries: bfloat16 [8192, 4096], P(('groups', 'seq', 'rep'), 'head'), parts along dimension 0, may hold values from -6 to 6
- keys: bfloat16 [8192, 4096], P(('groups', 'seq', 'rep'), 'head'), parts along dimension 0, may hold values from -6 to 6
- values: bfloat16 [8192, 4096], P(('groups', 'seq', 'rep'), 'head'), parts along dimension 0, may hold values from -6 to 6
- d_out: bfloat16 [8192, 4096], P(('groups', 'seq', 'rep'), 'head'), parts along dimension 0, may hold values from -6 to 6
- doc_lengths: int32 [16], P('groups'), parts along dimension 0, may hold values from 1 to 2048, 4096 in all
- gain: float32 [4096], P('head'), may hold values from 0.25 to 1.75
Outputs:
- mixed: bfloat16 [8192, 4096], P(('groups', 'seq', 'rep'), 'head'), parts along dimension 0
- grad_queries: bfloat16 [8192, 4096], P(('groups', 'seq', 'rep'), 'head'), parts along dimension 0
- grad_keys: bfloat16 [8192, 4096], P(('groups', 'seq', 'rep'), 'head'), parts along dimension 0
- grad_values: bfloat16 [8192, 4096], P(('groups', 'seq', 'rep'), 'head'), parts along dimension 0
- grad_gain: float32 [2, 4096], P('groups', 'head'), parts along dimension 0
The draws below stay inside these ranges and needn't reach their ends.
There are 2 independent parts, one for each index of `groups`. The reference program is written for one: setup_inputs(seed, part) draws one part's arguments, and reference() takes and returns one part's arrays. A program takes and returns all parts, laid end to end along the dimension named above; an argument that names none is the same for every part. Nothing has to cross between parts.
Inputs may be any that keep to these rules, and one draw needn't show every extreme that they name: `doc_lengths`: the entries sum to 4096, and the largest is exactly half of 4096.
All inputs are finite; a program needn't handle non-finite values.
Results may differ from the reference program's by a relative error of at most 0.0059.
Values sent between devices are 32-bit elements; how exact they have to be, the bound alone decides.
A program may use at most 128 MiB of HBM per device.

```python
import math
import jax
import jax.numpy as jnp
import numpy as np
from jax import lax

HEADS = 32
DH = 128
NDOC = 8
BLOCK = 512
LEN = 4096


def levels(own_key, shape, split, smallest, top_value):
    factor_of = 1.0
    for position, shards_of in split:
        draws = jax.random.uniform(jax.random.fold_in(jax.random.fold_in(own_key, 6), position), (shards_of,), jnp.float32, smallest / len(split), top_value / len(split))
        factor_of = factor_of * jnp.repeat(jnp.exp(draws), shape[position] // shards_of).reshape((-1,) + (1,) * (len(shape) - 1 - position))
    return factor_of


def split_up(amount, total, most, slope):
    portions = [(1 << 20) // math.isqrt(standing ** slope) + 1 for standing in range(2, amount + 1)]
    surplus, holding = total - most - (amount - 1), [1] * (amount - 1)
    while surplus > 0:
        candidates = [i for i in range(amount - 1) if holding[i] < most]
        whole, remaining = sum([portions[i] for i in candidates]), surplus
        for i in candidates:
            extra = min(most - holding[i], max(1, remaining * portions[i] // whole), surplus)
            holding[i] = holding[i] + extra
            surplus = surplus - extra
    return np.array([most] + holding)


def ragged_sizes(key, number_of, total, most, lean):
    if number_of == 2:
        one = jax.random.randint(key, (), max(1, total - most), min(most, total - 1) + 1)
        return jnp.stack([one, total - one])
    sizes = jnp.asarray(split_up(number_of, total, most, lean), jnp.int32)
    twos = (number_of - 1) // 2
    donor, receiver = sizes[1:1 + 2 * twos:2], sizes[2:2 + 2 * twos:2]
    margin = jnp.minimum(donor - 1, most - receiver)
    passed = jax.random.randint(jax.random.fold_in(key, 1), (twos,), 0, 1 << 20) % (margin + 1)
    sizes = sizes.at[1:1 + 2 * twos:2].set(donor - passed).at[2:2 + 2 * twos:2].set(receiver + passed)
    return sizes[jax.random.permutation(jax.random.fold_in(key, 2), number_of)]


def bell_draw(rng, dims, spread, most, cuts=(), held_as=jnp.bfloat16):
    array = spread * jax.random.normal(rng, dims, jnp.float32)
    if cuts:
        array = array * levels(rng, dims, cuts, -0.22, 0.18)
    return jnp.clip(array, -most, most).astype(held_as)


def setup_inputs(seed: int = 0, part: int = 0) -> dict:
    splits = jax.random.split(jax.random.key(seed), 7)
    part_splits = jax.random.split(jax.random.fold_in(splits[6], part), 7)
    queries = bell_draw(part_splits[0], (LEN, HEADS * DH), 1.0, 6.0, ((0, 8), (1, 2)))
    keys = bell_draw(part_splits[1], (LEN, HEADS * DH), 1.0, 6.0, ((0, 8), (1, 2)))
    values = bell_draw(part_splits[2], (LEN, HEADS * DH), 1.0, 6.0, ((0, 8), (1, 2)))
    d_out = bell_draw(part_splits[3], (LEN, HEADS * DH), 1.0, 6.0, ((0, 8), (1, 2)))
    doc_lengths = ragged_sizes(part_splits[4], NDOC, LEN, LEN // 2, 2).astype(jnp.int32)
    gain = jnp.clip(1.0 + 0.15 * jax.random.normal(splits[5], (HEADS * DH,), jnp.float32), 0.25, 1.75)
    return {"queries": queries, "keys": keys, "values": values, "d_out": d_out, "doc_lengths": doc_lengths, "gain": gain}


def doc_index(doc_ends, places):
    return lax.optimization_barrier(jnp.sum((doc_ends[None, :] <= places[:, None]).astype(jnp.int32), axis=1))

def rounded(value):
    return lax.optimization_barrier(value.astype(jnp.bfloat16)).astype(jnp.float32)

def same_doc(block_docs):
    places = jnp.arange(block_docs.shape[0])
    return (block_docs[:, None] == block_docs[None, :]) & (places[:, None] >= places[None, :])

def forward_block(state_in, inputs):
    query_blk, key_blk, value_blk, block_docs, prior_doc = inputs
    scores = jnp.einsum('thd,shd->hts', query_blk, key_blk) / DH
    weights = rounded(jnp.where(same_doc(block_docs)[None], scores, 0.0))
    inner_sum = jnp.einsum('hts,shd->thd', weights, value_blk)
    carried = jnp.einsum('thd,hde->the', query_blk, rounded(state_in)) / DH
    output = inner_sum + jnp.where((block_docs == prior_doc)[:, None, None], carried, 0.0)
    tail_mask = (block_docs == block_docs[-1]).astype(jnp.float32)
    local_sum = jnp.einsum('thd,the->hde', key_blk * tail_mask[:, None, None], value_blk)
    renewed = local_sum + jnp.where(block_docs[-1] == prior_doc, state_in, 0.0)
    return (renewed, (output, state_in))

def backward_block(grad_state, inputs):
    query_blk, key_blk, value_blk, grad_blk, block_docs, prior_doc, next_doc, state_in = inputs
    doc_mask = same_doc(block_docs)[None]
    scores = jnp.einsum('thd,shd->hts', query_blk, key_blk) / DH
    weights = rounded(jnp.where(doc_mask, scores, 0.0))
    grad_scores = jnp.einsum('the,she->hts', grad_blk, value_blk)
    grad_weights = rounded(jnp.where(doc_mask, grad_scores, 0.0))
    grad_query = jnp.einsum('hts,shd->thd', grad_weights, key_blk) / DH
    grad_key = jnp.einsum('hts,thd->shd', grad_weights, query_blk) / DH
    grad_value = jnp.einsum('hts,the->she', weights, grad_blk)
    from_state = jnp.einsum('the,hde->thd', grad_blk, rounded(state_in)) / DH
    grad_query = grad_query + jnp.where((block_docs == prior_doc)[:, None, None], from_state, 0.0)
    later_mask = (block_docs == next_doc)[:, None, None]
    state_low = rounded(grad_state)
    grad_key = grad_key + jnp.where(later_mask, jnp.einsum('she,hde->shd', value_blk, state_low) / DH, 0.0)
    grad_value = grad_value + jnp.where(later_mask, jnp.einsum('shd,hde->she', key_blk, state_low) / DH, 0.0)
    head_mask = (block_docs == block_docs[0]).astype(jnp.float32)
    local_sum = jnp.einsum('thd,the->hde', query_blk * head_mask[:, None, None], grad_blk)
    renewed = local_sum + jnp.where(block_docs[0] == next_doc, grad_state, 0.0)
    return (renewed, (grad_query, grad_key, grad_value))

def reference(queries, keys, values, d_out, doc_lengths, gain):
    blocks = LEN // BLOCK
    shaped = (blocks, BLOCK, HEADS, DH)
    gains = gain.astype(jnp.float32).reshape(HEADS, DH)
    doc_ends = jnp.cumsum(doc_lengths).astype(jnp.int32)
    docs = doc_index(doc_ends, jnp.arange(LEN, dtype=jnp.int32))
    doc_blks = docs.reshape(blocks, BLOCK)
    priors = jnp.concatenate([doc_index(doc_ends, jnp.full((1,), -1, jnp.int32)), doc_blks[:-1, -1]])
    nexts = jnp.concatenate([doc_blks[1:, 0], doc_index(doc_ends, jnp.full((1,), LEN, jnp.int32))])
    query_blks = queries.astype(jnp.float32).reshape(shaped)
    key_blks = keys.astype(jnp.float32).reshape(shaped)
    value_blks = values.astype(jnp.float32).reshape(shaped)
    zero_state = jnp.zeros((HEADS, DH, DH), jnp.float32)
    final_state, (outputs, states) = lax.scan(forward_block, zero_state, (query_blks, key_blks, value_blks, doc_blks, priors))
    mean_sq = lax.optimization_barrier(jnp.mean(outputs * outputs, axis=-1, keepdims=True))
    inverse = lax.rsqrt(mean_sq + 1e-05)
    normed = outputs * inverse
    mixed = (normed * gains).astype(jnp.bfloat16)
    grad_out = d_out.astype(jnp.float32).reshape(shaped)
    gain_terms = lax.optimization_barrier(jnp.sum(grad_out * normed, axis=(0, 1)))
    grad_normed = grad_out * gains
    grad_attn = rounded(inverse * (grad_normed - normed * lax.optimization_barrier(jnp.mean(grad_normed * normed, axis=-1, keepdims=True))))
    final_grad, (grad_q, grad_k, grad_v) = lax.scan(backward_block, zero_state, (query_blks, key_blks, value_blks, grad_attn, doc_blks, priors, nexts, states), reverse=True)
    flat = (LEN, HEADS * DH)
    grad_gain = (gain_terms / math.sqrt(LEN)).reshape(1, HEADS * DH)
    return (mixed.reshape(flat), grad_q.astype(jnp.bfloat16).reshape(flat), grad_k.astype(jnp.bfloat16).reshape(flat), grad_v.astype(jnp.bfloat16).reshape(flat), grad_gain)
```

```python
import functools
import math

import jax
import jax.numpy as jnp
from jax import lax
from jax.experimental import pallas as pl
from jax.experimental.pallas import tpu as pltpu
from jax.sharding import PartitionSpec as P

DH = 128
PAIR = 2 * DH
HALF = 256
MESH = pl.DeviceIdType.MESH
F32 = jnp.float32
BF16 = jnp.bfloat16
TOP, BOT = slice(0, HALF), slice(HALF, 2 * HALF)
HALVES = (TOP, BOT)
SIDES = (slice(0, DH), slice(DH, PAIR))

UNITS = "ABFCKDG"
ORDERS = {
    (4, 8): (
        "AAAAAFFFAFFAAFBCFFBCBCBCBCBCBCBCGKDKDKDKKDDKDKKDD",
        "AAAAAAAABBBBFBBFCBFCBFCFCFCCFFCCGKDKDKKDDKDKKDDKD",
        "AAAAAAAABBBBBBBBFCFFCFCCFFCKFCDFKCCKGDKDDKKDKDDKD",
        "AAAAAAAABBBBBBBBFCFKCFDFKCFCFKCFKCKCFKDKCGDKDDDDD",
    ),
}


def orders_of(seqs, pairs):
    plain = "A" * pairs + "B" * pairs + "FC" * pairs + "G" + "KD" * pairs
    return ORDERS.get((seqs, pairs), (plain,) * seqs)


def nn(a, b):
    return lax.dot_general(a, b, (((1,), (0,)), ((), ())), preferred_element_type=F32)


def nt(a, b):
    return lax.dot_general(a, b, (((1,), (1,)), ((), ())), preferred_element_type=F32)


def tn(a, b):
    return lax.dot_general(a, b, (((0,), (0,)), ((), ())), preferred_element_type=F32)


def kernel(
    pairs, tokens, seqs, reps, ndoc,
    lens_hbm, gain_hbm, q_hbm, k_hbm, v_hbm, d_hbm,
    mix, gq, gk, gv, ggain,
    lens, gain, qs, ks, vs, ds, acc, ws, gs, mask, fwd_m, bwd_m, tail_m, head_m,
    fown, fhalf, fpart, fin, fout, frel, fstate,
    bown, bhalf, bpart, bin_, bout, brel, bstate,
    sb, gsb, gslots,
    in_sem, small_sem, fsem, bsem, gsend, grecv,
):
    n = seqs * reps
    chip, core = lax.axis_index("seq"), lax.axis_index("rep")
    rank = chip * reps + core
    total = n * tokens
    first = rank * tokens
    middle = first + HALF

    def device(other):
        return {"seq": lax.div(other, reps), "rep": lax.rem(other, reps)}

    def cols(p):
        return pl.ds(pl.multiple_of(p * PAIR, PAIR), PAIR)

    def load(i, hbm, buf, p):
        return pltpu.make_async_copy(hbm.at[:, cols(p)], buf.at[p], in_sem.at[i, p])

    def each(fn):
        lax.fori_loop(0, pairs, lambda p, c: (fn(p), c)[1], 0)

    def start_kv(p):
        load(0, k_hbm, ks, p).start()
        load(1, v_hbm, vs, p).start()

    def start_qd(p):
        load(2, q_hbm, qs, p).start()
        load(3, d_hbm, ds, p).start()

    lens_copy = pltpu.make_async_copy(lens_hbm, lens, small_sem.at[0])
    gain_copy = pltpu.make_async_copy(gain_hbm, gain, small_sem.at[1])
    lens_copy.start()
    gain_copy.start()
    each(start_kv)
    each(start_qd)
    barrier = pltpu.get_barrier_semaphore()
    for o in range(1, n):
        pl.semaphore_signal(barrier, inc=1, device_id=device(lax.rem(rank + o, n)), device_id_type=MESH)

    lens_copy.wait()
    gain_copy.wait()

    ends = []
    run = jnp.int32(0)
    for i in range(ndoc):
        run = run + lens[i]
        ends.append(run)

    def doc_of(place):
        return sum((jnp.where(e <= place, 1, 0) for e in ends))

    before, after = doc_of(first - 1), doc_of(first + tokens)
    doc_first, doc_last = doc_of(first), doc_of(first + tokens - 1)
    doc_up, doc_down = doc_of(middle - 1), doc_of(middle)
    col = lax.broadcasted_iota(jnp.int32, (HALF, DH), 0)
    place_row = lax.broadcasted_iota(jnp.int32, (8, HALF), 1)

    def spread(ref, s, hit):
        ones = jnp.where(hit, 1.0, 0.0).astype(BF16)
        for side in SIDES:
            ref[HALVES[s], side] = ones

    for s in range(2):
        doc_col = doc_of(col + (first + s * HALF))
        spread(fwd_m, s, doc_col == (doc_up if s else before))
        spread(bwd_m, s, doc_col == (after if s else doc_down))
        spread(tail_m, s, doc_col == (doc_last if s else doc_up))
        spread(head_m, s, doc_col == (doc_down if s else doc_first))
        doc_row = doc_of(place_row + (first + s * HALF))
        for side in SIDES:
            keep = (doc_col == doc_row[0:1, side]) & (col >= place_row[0:1, side])
            mask[s, :, side] = jnp.where(keep, 1.0 / DH, 0.0)

    def same(one, other):
        return jnp.where(one == other, 1.0, 0.0)

    def carries(one, other):
        return same(doc_of(one), doc_of(other))

    up_last, up_before = same(doc_up, doc_last), same(doc_up, before)
    down_first, down_after = same(doc_down, doc_first), same(doc_down, after)

    base = chip * reps * tokens
    flags_f = [carries(base + i * tokens - 1, base + (i + 1) * tokens - 1) for i in range(2)]
    flags_b = [carries(base + i * tokens, base + (i + 1) * tokens) for i in (1, 0)]

    @pl.when(chip == 0)
    def _():
        fin[...] = jnp.zeros_like(fin)

    @pl.when(chip == seqs - 1)
    def _():
        bin_[...] = jnp.zeros_like(bin_)

    def clear(p):
        for s in range(2):
            for i in range(2):
                sb[p, s, SIDES[i], SIDES[1 - i]] = jnp.zeros((DH, DH), BF16)

    each(clear)
    for s in range(2):
        for i in range(2):
            gsb[s, SIDES[i], SIDES[1 - i]] = jnp.zeros((DH, DH), BF16)

    other_core = {"rep": 1 - core}

    class Chain:
        def __init__(self, own, part, arrived, out, rel, state, sems, late, flags, ends, onward):
            self.own, self.part, self.arrived, self.out = own, part, arrived, out
            self.rel, self.state, self.sems = rel, state, sems
            f0, f1 = flags
            self.c_own, self.c_part = jnp.where(late, 1.0, f1), jnp.where(late, f1, 1.0)
            self.c_in = f0 * f1
            self.own_part, self.own_in = jnp.where(late, 1.0, 0.0), jnp.where(late, f0, 1.0)
            self.rel_own, self.rel_in = jnp.where(late, 0.0, 1.0), jnp.where(late, 1.0, f0)
            self.is_first, self.is_last = ends
            self.onward = onward

        def remote(self, src, dst, kind, p, where):
            return pltpu.make_async_remote_copy(
                src_ref=src, dst_ref=dst, send_sem=self.sems.at[kind, 0, p], recv_sem=self.sems.at[kind, 1, p],
                device_id=where, device_id_type=MESH,
            )

        def to_partner(self, p):
            return self.remote(self.own.at[2 * p + 1 - core], self.part.at[p], 0, p, other_core)

        def to_next(self, p):
            return self.remote(self.out.at[p], self.arrived.at[p], 1, p, self.onward)

        def relay(self, p):
            return self.remote(self.rel.at[p], self.state.at[2 * p + core], 2, p, other_core)

        def step(self, p):
            self.to_partner(p).wait_recv()

            @pl.when(jnp.logical_not(self.is_first))
            def _():
                self.to_next(p).wait_recv()

            own, part, came = self.own[2 * p + core], self.part[p], self.arrived[p]

            @pl.when(jnp.logical_not(self.is_last))
            def _():
                self.out[p] = self.c_own * own + self.c_part * part + self.c_in * came
                self.to_next(p).start()

            self.rel[p] = self.rel_own * own + self.rel_in * came
            self.relay(p).start()
            self.state[2 * p + core] = self.own_part * part + self.own_in * came

        def take(self, p):
            self.remote(self.rel.at[p], self.state.at[2 * p + 1 - core], 2, p, other_core).wait_recv()

        def finish(self, p):
            self.to_partner(p).wait_send()
            self.relay(p).wait_send()

            @pl.when(jnp.logical_not(self.is_last))
            def _():
                self.to_next(p).wait_send()

    ahead = Chain(
        fown, fpart, fin, fout, frel, fstate, fsem, core == 1, flags_f,
        (chip == 0, chip == seqs - 1), {"seq": jnp.minimum(chip + 1, seqs - 1)},
    )
    back = Chain(
        bown, bpart, bin_, bout, brel, bstate, bsem, core == 0, flags_b,
        (chip == seqs - 1, chip == 0), {"seq": jnp.maximum(chip - 1, 0)},
    )

    pl.semaphore_wait(barrier, n - 1)

    def local(p):
        load(0, k_hbm, ks, p).wait()
        load(1, v_hbm, vs, p).wait()
        sums = [tn(ks[p, s] * tail_m[s], vs[p, s]) for s in HALVES]
        for i, side in enumerate(SIDES):
            up, low = (x[side, side] for x in sums)
            fhalf[2 * p + i] = up
            fown[2 * p + i] = low + up_last * up
        ahead.to_partner(p).start()

    PLACES = [(s, i) for s in range(2) for i in range(2)]

    def scores(p):
        load(2, q_hbm, qs, p).wait()
        raw = [nt(qs[p, HALVES[s], SIDES[i]], ks[p, HALVES[s], SIDES[i]]) for s, i in PLACES]
        kept = [(x * mask[s]).astype(BF16) for x, (s, i) in zip(raw, PLACES)]
        sums = [nn(w, vs[p, HALVES[s], SIDES[i]]) for w, (s, i) in zip(kept, PLACES)]
        for w, x, (s, i) in zip(kept, sums, PLACES):
            ws[p, s, i] = w
            acc[p, HALVES[s], SIDES[i]] = x

    def forward(p):
        ahead.take(p)
        load(3, d_hbm, ds, p).wait()
        for i, side in enumerate(SIDES):
            state = fstate[2 * p + i]
            sb[p, 0, side, side] = (state * (1.0 / DH)).astype(BF16)
            sb[p, 1, side, side] = ((up_before * state + fhalf[2 * p + i]) * (1.0 / DH)).astype(BF16)
        carried = [nn(qs[p, HALVES[s]] * fwd_m[HALVES[s]], sb[p, s]) for s in range(2)]
        gains = [gain[pl.ds(2 * p + i, 1), :] for i in range(2)]
        made = []
        for s, i in PLACES:
            half, side = HALVES[s], SIDES[i]
            attn = acc[p, half, side] + carried[s][:, side]
            inverse = lax.rsqrt(jnp.mean(attn * attn, axis=-1, keepdims=True) + 1e-5)
            normed = attn * inverse
            mixed = (normed * gains[i]).astype(BF16)
            d = ds[p, half, side].astype(F32)
            terms = jnp.sum(d * normed, axis=0, keepdims=True)
            g = d * gains[i]
            inner = jnp.mean(g * normed, axis=-1, keepdims=True)
            made.append((mixed, (inverse * (g - normed * inner)).astype(BF16), terms))
        for (s, i), (mixed, grad, terms) in zip(PLACES, made):
            mix[HALVES[s], pl.ds(pl.multiple_of(p * PAIR + i * DH, DH), DH)] = mixed
            gs[p, HALVES[s], SIDES[i]] = grad
        for i, side in enumerate(SIDES):
            gslots[rank, pl.ds(2 * p + i, 1), :] = made[i][2] + made[2 + i][2]
        sums = [tn(qs[p, s] * head_m[s], gs[p, s]) for s in HALVES]
        for i, side in enumerate(SIDES):
            up, low = (x[side, side] for x in sums)
            bhalf[2 * p + i] = low
            bown[2 * p + i] = up + down_first * low
        back.to_partner(p).start()

    def grads(p):
        back.take(p)
        for i, side in enumerate(SIDES):
            state = bstate[2 * p + i]
            gsb[1, side, side] = (state * (1.0 / DH)).astype(BF16)
            gsb[0, side, side] = ((down_after * state + bhalf[2 * p + i]) * (1.0 / DH)).astype(BF16)
        raw = [nt(gs[p, HALVES[s], SIDES[i]], vs[p, HALVES[s], SIDES[i]]) for s, i in PLACES]
        kept = [(x * mask[s]).astype(BF16) for x, (s, i) in zip(raw, PLACES)]
        to_q = [nt(gs[p, HALVES[s]] * fwd_m[HALVES[s]], sb[p, s]) for s in range(2)]
        to_k = [nt(vs[p, HALVES[s]] * bwd_m[HALVES[s]], gsb[s]) for s in range(2)]
        to_v = [nn(ks[p, HALVES[s]] * bwd_m[HALVES[s]], gsb[s]) for s in range(2)]
        made = []
        for g, (s, i) in zip(kept, PLACES):
            half, side = HALVES[s], SIDES[i]
            made.append((
                (nn(g, ks[p, half, side]) + to_q[s][:, side]).astype(BF16),
                (tn(g, qs[p, half, side]) + to_k[s][:, side]).astype(BF16),
                (tn(ws[p, s, i], gs[p, half, side]) + to_v[s][:, side]).astype(BF16),
            ))
        for (s, i), values in zip(PLACES, made):
            for ref, value in zip((gq, gk, gv), values):
                ref[HALVES[s], pl.ds(pl.multiple_of(p * PAIR + i * DH, DH), DH)] = value

    def gcopy(o):
        return pltpu.make_async_remote_copy(
            src_ref=gslots.at[rank], dst_ref=gslots.at[rank], send_sem=gsend.at[o], recv_sem=grecv.at[rank],
            device_id=device(lax.rem(rank + o, n)), device_id_type=MESH,
        )

    def share_gain(p):
        for o in range(1, n):
            gcopy(o).start()

    orders = orders_of(seqs, pairs)
    steps = max(len(order) for order in orders)
    words = []
    for at in range(0, steps, 10):
        word = jnp.int32(0)
        for c, order in enumerate(orders):
            bits = sum(
                (UNITS.index(order[at + j]) if at + j < len(order) else 7) << (3 * j) for j in range(min(10, steps - at))
            )
            word = jnp.where(chip == c, jnp.int32(bits), word)
        words.append(word)
    work = (local, scores, ahead.step, forward, back.step, grads, share_gain)

    def step(i, counts):
        group = lax.div(i, 10)
        word = words[0]
        for g in range(1, len(words)):
            word = jnp.where(group == g, words[g], word)
        unit = lax.shift_right_logical(word, 3 * lax.rem(i, 10)) & 7
        for u, fn in enumerate(work):
            pl.when(unit == u)(functools.partial(fn, counts[u]))
        return tuple(count + jnp.where(unit == u, 1, 0) for u, count in enumerate(counts))

    lax.fori_loop(0, steps, step, (jnp.int32(0),) * len(work))

    for o in range(1, n):
        src = lax.rem(rank + n - o, n)
        pltpu.make_async_remote_copy(
            src_ref=gslots.at[src], dst_ref=gslots.at[src], send_sem=gsend.at[o], recv_sem=grecv.at[src],
            device_id=device(src), device_id_type=MESH,
        ).wait_recv()
        gcopy(o).wait_send()
    summed = gslots[0]
    for i in range(1, n):
        summed = summed + gslots[i]
    ggain[...] = summed * (1.0 / math.sqrt(total))

    def finish(p):
        ahead.finish(p)
        back.finish(p)

    each(finish)


def writer(*refs):
    count = len(refs) // 2
    sems = refs[-1]
    copies = [pltpu.make_async_copy(refs[i], refs[count + i], sems.at[i]) for i in range(count)]
    for copy in copies:
        copy.start()
    for copy in copies:
        copy.wait()


def shards(queries, keys, values, d_out, doc_lengths, gain):
    tokens, width = queries.shape
    pairs = width // PAIR
    heads = 2 * pairs
    seqs, reps = lax.axis_size("seq"), lax.axis_size("rep")
    n = seqs * reps
    slab = pltpu.VMEM((pairs, tokens, PAIR), BF16)
    rows = pltpu.VMEM((tokens, PAIR), BF16)
    state = pltpu.VMEM((heads, DH, DH), F32)
    half = pltpu.VMEM((pairs, DH, DH), F32)
    dma = pltpu.SemaphoreType.DMA
    big = jax.ShapeDtypeStruct((tokens, width), BF16)
    hbm = pl.BlockSpec(memory_space=pltpu.HBM)
    vmem = pl.BlockSpec(memory_space=pltpu.VMEM)
    shapes = (big, big, big, big, jax.ShapeDtypeStruct((heads, DH), F32))
    out = pl.pallas_call(
        functools.partial(kernel, pairs, tokens, seqs, reps, doc_lengths.shape[0]),
        out_shape=shapes,
        in_specs=[hbm] * 6,
        out_specs=(vmem,) * 5,
        scratch_shapes=[
            pltpu.SMEM(doc_lengths.shape, jnp.int32),
            pltpu.VMEM((heads, DH), F32),
            slab, slab, slab, slab,
            pltpu.VMEM((pairs, tokens, PAIR), F32),
            pltpu.VMEM((pairs, 2, 2, HALF, HALF), BF16),
            slab,
            pltpu.VMEM((2, HALF, HALF), F32),
            rows, rows, rows, rows,
            state, state, half, half, half, half, state,
            state, state, half, half, half, half, state,
            pltpu.VMEM((pairs, 2, PAIR, PAIR), BF16),
            pltpu.VMEM((2, PAIR, PAIR), BF16),
            pltpu.VMEM((n, heads, DH), F32),
            dma((4, pairs)), dma((2,)), dma((3, 2, pairs)), dma((3, 2, pairs)),
            dma((n,)), dma((n,)),
        ],
        compiler_params=pltpu.CompilerParams(
            collective_id=0, has_side_effects=True, vmem_limit_bytes=44 << 20
        ),
    )(doc_lengths, gain.reshape(heads, DH), queries, keys, values, d_out)
    out = pl.pallas_call(
        writer,
        out_shape=shapes,
        in_specs=[pl.BlockSpec(memory_space=pl.ANY)] * 5,
        out_specs=(hbm,) * 5,
        scratch_shapes=[dma((5,))],
        compiler_params=pltpu.CompilerParams(vmem_limit_bytes=1 << 20),
    )(*out)
    return (*out[:4], out[4].reshape(1, width))


def solution(mesh):
    token = P(("groups", "seq", "rep"), "head")
    return jax.shard_map(
        shards,
        mesh=mesh,
        in_specs=(token, token, token, token, P("groups"), P("head")),
        out_specs=(token, token, token, token, P("groups", "head")),
        check_vma=False,
    )
```

```python
import functools
import math

import jax
import jax.numpy as jnp
from jax import lax
from jax.experimental import pallas as pl
from jax.experimental.pallas import tpu as pltpu
from jax.sharding import PartitionSpec as P

DH = 128
PAIR = 2 * DH
HALF = 256
MESH = pl.DeviceIdType.MESH
F32 = jnp.float32
BF16 = jnp.bfloat16
TOP, BOT = slice(0, HALF), slice(HALF, 2 * HALF)
HALVES = (TOP, BOT)
SIDES = (slice(0, DH), slice(DH, PAIR))

UNITS = "ABFCKDGEHLM"
PLANS = {
    (4, 8): (
        (1, 4, 5, 7),
        (0, 2, 3, 6),
        (
            (
                "A0A1A2A5A6A4A3F0F2F6H1H5F3H4A7B1C1H7B5C5B6C6B0C0B2C2B4C4B3C3",
                "B7C7G0M0D0M2D2M6D6K1D1K5M3D5D3K4K7D4D7",
            ),
            (
                "A0A1A4A5B0B1E4E1E5B4B5A2B2A3B3A6B6A7F0B7E7F2C0C2F6H1C6H5C1F3",
                "C5H4C3H7C4L0C7G0L2L6K1D1K5L3D5K4D4K7M2D7M0D2M6D0M3D6D3",
            ),
            (
                "A0A1A3A6B0B1B6B3A7B7A2B2A4B4A5B5E4E1E5F0C0E7F2L0C2F6H1L2C6H5",
                "C1L6F3C5K1H4C3K5H7C4L3C7G0K4D1K7M2D4D7M0D2M6D0M3D6D5D3",
            ),
            (
                "A0A2A1A5B0B2B5B1A7B7A6B6A3B3A4B4H4C4H1H5K4C1F0C5K1C0K5H7F2D1",
                "C7F6C2K7C6M2M0F3D5M6C3G0D2M3D7D6D0D3D4",
            ),
        ),
    ),
}
SLOTS = 4


def plan_of(seqs, pairs):
    every = range(pairs)
    plain = [("A", p) for p in every] + [("B", p) for p in every] + [(u, p) for p in every for u in "FC"]
    plain += [("G", 0)] + [(u, p) for p in every for u in "KD"]
    if (seqs, pairs) not in PLANS:
        return (), (), (plain,) * seqs
    ahead, back, orders = PLANS[seqs, pairs]
    texts = ["".join(parts) for parts in orders]
    return ahead, back, [[(t[i], int(t[i + 1])) for i in range(0, len(t), 2)] for t in texts]


def nn(a, b):
    return lax.dot_general(a, b, (((1,), (0,)), ((), ())), preferred_element_type=F32)


def nt(a, b):
    return lax.dot_general(a, b, (((1,), (1,)), ((), ())), preferred_element_type=F32)


def tn(a, b):
    return lax.dot_general(a, b, (((0,), (0,)), ((), ())), preferred_element_type=F32)


def kernel(
    pairs, tokens, seqs, reps, ndoc,
    lens_hbm, gain_hbm, q_hbm, k_hbm, v_hbm, d_hbm,
    mix, gq, gk, gv, ggain,
    lens, gain, qs, ks, vs, ds, acc, ws, gs, mask, fwd_m, bwd_m, tail_m, head_m,
    fown, fhalf, fpart, fin, fin2, fout, fout2, frel, fstate,
    bown, bhalf, bpart, bin_, bin2, bout, bout2, brel, bstate,
    sb, gsb, gslots,
    in_sem, small_sem, fsem, bsem, gsend, grecv,
):
    n = seqs * reps
    chip, core = lax.axis_index("seq"), lax.axis_index("rep")
    rank = chip * reps + core
    total = n * tokens
    first = rank * tokens
    middle = first + HALF

    def device(other):
        return {"seq": lax.div(other, reps), "rep": lax.rem(other, reps)}

    def cols(p):
        return pl.ds(pl.multiple_of(p * PAIR, PAIR), PAIR)

    def load(i, hbm, buf, p):
        return pltpu.make_async_copy(hbm.at[:, cols(p)], buf.at[p], in_sem.at[i, p])

    def each(fn):
        lax.fori_loop(0, pairs, lambda p, c: (fn(p), c)[1], 0)

    def start_kv(p):
        load(0, k_hbm, ks, p).start()
        load(1, v_hbm, vs, p).start()

    def start_qd(p):
        load(2, q_hbm, qs, p).start()
        load(3, d_hbm, ds, p).start()

    lens_copy = pltpu.make_async_copy(lens_hbm, lens, small_sem.at[0])
    gain_copy = pltpu.make_async_copy(gain_hbm, gain, small_sem.at[1])
    lens_copy.start()
    gain_copy.start()
    each(start_kv)
    each(start_qd)
    barrier = pltpu.get_barrier_semaphore()
    for o in range(1, n):
        pl.semaphore_signal(barrier, inc=1, device_id=device(lax.rem(rank + o, n)), device_id_type=MESH)

    lens_copy.wait()
    gain_copy.wait()

    ends = []
    run = jnp.int32(0)
    for i in range(ndoc):
        run = run + lens[i]
        ends.append(run)

    def doc_of(place):
        return sum((jnp.where(e <= place, 1, 0) for e in ends))

    before, after = doc_of(first - 1), doc_of(first + tokens)
    doc_first, doc_last = doc_of(first), doc_of(first + tokens - 1)
    doc_up, doc_down = doc_of(middle - 1), doc_of(middle)
    col = lax.broadcasted_iota(jnp.int32, (HALF, DH), 0)
    place_row = lax.broadcasted_iota(jnp.int32, (8, HALF), 1)

    def spread(ref, s, hit):
        ones = jnp.where(hit, 1.0, 0.0).astype(BF16)
        for side in SIDES:
            ref[HALVES[s], side] = ones

    for s in range(2):
        doc_col = doc_of(col + (first + s * HALF))
        spread(fwd_m, s, doc_col == (doc_up if s else before))
        spread(bwd_m, s, doc_col == (after if s else doc_down))
        spread(tail_m, s, doc_col == (doc_last if s else doc_up))
        spread(head_m, s, doc_col == (doc_down if s else doc_first))
        doc_row = doc_of(place_row + (first + s * HALF))
        for side in SIDES:
            keep = (doc_col == doc_row[0:1, side]) & (col >= place_row[0:1, side])
            mask[s, :, side] = jnp.where(keep, 1.0 / DH, 0.0)

    def same(one, other):
        return jnp.where(one == other, 1.0, 0.0)

    def carries(one, other):
        return same(doc_of(one), doc_of(other))

    up_last, up_before = same(doc_up, doc_last), same(doc_up, before)
    down_first, down_after = same(doc_down, doc_first), same(doc_down, after)

    base = chip * reps * tokens
    flags_f = [carries(base + i * tokens - 1, base + (i + 1) * tokens - 1) for i in range(2)]
    flags_b = [carries(base + i * tokens, base + (i + 1) * tokens) for i in (1, 0)]

    @pl.when(chip == 0)
    def _():
        fin[...] = jnp.zeros_like(fin)

    @pl.when(chip == seqs - 1)
    def _():
        bin_[...] = jnp.zeros_like(bin_)

    split_f, split_b, orders = plan_of(seqs, pairs)

    for split, place, later in ((split_f, chip, fin2), (split_b, seqs - 1 - chip, bin2)):
        if split:
            @pl.when(place != 2)
            def _():
                later[...] = jnp.zeros_like(later)

    def clear(p):
        for s in range(2):
            for i in range(2):
                sb[p, s, SIDES[i], SIDES[1 - i]] = jnp.zeros((DH, DH), BF16)

    each(clear)
    for s in range(2):
        for i in range(2):
            gsb[s, SIDES[i], SIDES[1 - i]] = jnp.zeros((DH, DH), BF16)

    other_core = {"rep": 1 - core}

    class Chain:
        def __init__(self, own, part, arrived, arrived2, out, out2, rel, state, sems, late, flags, place, onward, split):
            self.own, self.part, self.arrived, self.arrived2 = own, part, arrived, arrived2
            self.out, self.out2, self.rel, self.state, self.sems = out, out2, rel, state, sems
            f0, f1 = flags
            self.c_own, self.c_part = jnp.where(late, 1.0, f1), jnp.where(late, f1, 1.0)
            self.c_in = f0 * f1
            self.own_part, self.own_in = jnp.where(late, 1.0, 0.0), jnp.where(late, f0, 1.0)
            self.rel_own, self.rel_in = jnp.where(late, 0.0, 1.0), jnp.where(late, 1.0, f0)
            self.place, self.onward = place, onward
            self.is_first, self.is_last = place == 0, place == seqs - 1
            self.split = sum(1 << p for p in split)

        def remote(self, src, dst, kind, p, where):
            return pltpu.make_async_remote_copy(
                src_ref=src, dst_ref=dst, send_sem=self.sems.at[kind, 0, p], recv_sem=self.sems.at[kind, 1, p],
                device_id=where, device_id_type=MESH,
            )

        def to_partner(self, p):
            return self.remote(self.own.at[2 * p + 1 - core], self.part.at[p], 0, p, other_core)

        def to_next(self, p):
            return self.remote(self.out.at[p], self.arrived.at[p], 1, p, self.onward)

        def relay(self, p):
            return self.remote(self.rel.at[p], self.state.at[2 * p + core], 2, p, other_core)

        def after(self, p):
            return self.remote(self.out2.at[p], self.arrived2.at[p], 3, p, self.onward)

        def keep(self, p, own, part, came):
            self.rel[p] = self.rel_own * own + self.rel_in * came
            self.relay(p).start()
            self.state[2 * p + core] = self.own_part * part + self.own_in * came

        def step(self, p):
            self.to_partner(p).wait_recv()

            @pl.when(jnp.logical_not(self.is_first))
            def _():
                self.to_next(p).wait_recv()

            own, part, came = self.own[2 * p + core], self.part[p], self.arrived[p]

            @pl.when(jnp.logical_not(self.is_last))
            def _():
                self.out[p] = self.c_own * own + self.c_part * part + self.c_in * came
                self.to_next(p).start()

            self.keep(p, own, part, came)

        def early(self, p):
            self.to_partner(p).wait_recv()
            both = self.c_own * self.own[2 * p + core] + self.c_part * self.part[p]

            @pl.when(self.place == 1)
            def _():
                self.out[p] = both

            @pl.when(self.place == 2)
            def _():
                self.to_next(p).wait_recv()
                self.out[p] = both + self.c_in * self.arrived[p]

            self.to_next(p).start()

        def rest(self, p):
            @pl.when(self.is_first | self.is_last)
            def _():
                self.to_partner(p).wait_recv()

            @pl.when((self.place == 1) | self.is_last)
            def _():
                self.to_next(p).wait_recv()

            @pl.when(self.is_first)
            def _():
                self.out[p] = self.c_own * self.own[2 * p + core] + self.c_part * self.part[p]
                self.to_next(p).start()

            @pl.when(self.place == 1)
            def _():
                self.out2[p] = self.c_in * self.arrived[p]
                self.after(p).start()

            @pl.when(self.place == 2)
            def _():
                self.after(p).wait_recv()

            self.keep(p, self.own[2 * p + core], self.part[p], self.arrived[p] + self.arrived2[p])

        def take(self, p):
            self.remote(self.rel.at[p], self.state.at[2 * p + 1 - core], 2, p, other_core).wait_recv()

        def finish(self, p):
            self.to_partner(p).wait_send()
            self.relay(p).wait_send()

            @pl.when(jnp.logical_not(self.is_last))
            def _():
                self.to_next(p).wait_send()

            if self.split:
                other_way = lax.shift_right_logical(jnp.int32(self.split), p) & 1

                @pl.when((self.place == 1) & (other_way == 1))
                def _():
                    self.after(p).wait_send()

    ahead = Chain(
        fown, fpart, fin, fin2, fout, fout2, frel, fstate, fsem, core == 1, flags_f,
        chip, {"seq": jnp.minimum(chip + 1, seqs - 1)}, split_f,
    )
    back = Chain(
        bown, bpart, bin_, bin2, bout, bout2, brel, bstate, bsem, core == 0, flags_b,
        seqs - 1 - chip, {"seq": jnp.maximum(chip - 1, 0)}, split_b,
    )

    def local(p):
        load(0, k_hbm, ks, p).wait()
        load(1, v_hbm, vs, p).wait()
        sums = [tn(ks[p, s] * tail_m[s], vs[p, s]) for s in HALVES]
        for i, side in enumerate(SIDES):
            up, low = (x[side, side] for x in sums)
            fhalf[2 * p + i] = up
            fown[2 * p + i] = low + up_last * up

    PLACES = [(s, i) for s in range(2) for i in range(2)]

    def scores(p):
        load(2, q_hbm, qs, p).wait()
        raw = [nt(qs[p, HALVES[s], SIDES[i]], ks[p, HALVES[s], SIDES[i]]) for s, i in PLACES]
        kept = [(x * mask[s]).astype(BF16) for x, (s, i) in zip(raw, PLACES)]
        sums = [nn(w, vs[p, HALVES[s], SIDES[i]]) for w, (s, i) in zip(kept, PLACES)]
        for w, x, (s, i) in zip(kept, sums, PLACES):
            ws[p, s, i] = w
            acc[p, HALVES[s], SIDES[i]] = x

    def forward(p):
        ahead.take(p)
        load(3, d_hbm, ds, p).wait()
        for i, side in enumerate(SIDES):
            state = fstate[2 * p + i]
            sb[p, 0, side, side] = (state * (1.0 / DH)).astype(BF16)
            sb[p, 1, side, side] = ((up_before * state + fhalf[2 * p + i]) * (1.0 / DH)).astype(BF16)
        carried = [nn(qs[p, HALVES[s]] * fwd_m[HALVES[s]], sb[p, s]) for s in range(2)]
        gains = [gain[pl.ds(2 * p + i, 1), :] for i in range(2)]
        made = []
        for s, i in PLACES:
            half, side = HALVES[s], SIDES[i]
            attn = acc[p, half, side] + carried[s][:, side]
            inverse = lax.rsqrt(jnp.mean(attn * attn, axis=-1, keepdims=True) + 1e-5)
            normed = attn * inverse
            mixed = (normed * gains[i]).astype(BF16)
            d = ds[p, half, side].astype(F32)
            terms = jnp.sum(d * normed, axis=0, keepdims=True)
            g = d * gains[i]
            inner = jnp.mean(g * normed, axis=-1, keepdims=True)
            made.append((mixed, (inverse * (g - normed * inner)).astype(BF16), terms))
        for (s, i), (mixed, grad, terms) in zip(PLACES, made):
            mix[HALVES[s], pl.ds(pl.multiple_of(p * PAIR + i * DH, DH), DH)] = mixed
            gs[p, HALVES[s], SIDES[i]] = grad
        for i, side in enumerate(SIDES):
            gslots[rank, pl.ds(2 * p + i, 1), :] = made[i][2] + made[2 + i][2]
        sums = [tn(qs[p, s] * head_m[s], gs[p, s]) for s in HALVES]
        for i, side in enumerate(SIDES):
            up, low = (x[side, side] for x in sums)
            bhalf[2 * p + i] = low
            bown[2 * p + i] = up + down_first * low
        back.to_partner(p).start()

    def grads(p):
        back.take(p)
        for i, side in enumerate(SIDES):
            state = bstate[2 * p + i]
            gsb[1, side, side] = (state * (1.0 / DH)).astype(BF16)
            gsb[0, side, side] = ((down_after * state + bhalf[2 * p + i]) * (1.0 / DH)).astype(BF16)
        raw = [nt(gs[p, HALVES[s], SIDES[i]], vs[p, HALVES[s], SIDES[i]]) for s, i in PLACES]
        kept = [(x * mask[s]).astype(BF16) for x, (s, i) in zip(raw, PLACES)]
        to_q = [nt(gs[p, HALVES[s]] * fwd_m[HALVES[s]], sb[p, s]) for s in range(2)]
        to_k = [nt(vs[p, HALVES[s]] * bwd_m[HALVES[s]], gsb[s]) for s in range(2)]
        to_v = [nn(ks[p, HALVES[s]] * bwd_m[HALVES[s]], gsb[s]) for s in range(2)]
        made = []
        for g, (s, i) in zip(kept, PLACES):
            half, side = HALVES[s], SIDES[i]
            made.append((
                (nn(g, ks[p, half, side]) + to_q[s][:, side]).astype(BF16),
                (tn(g, qs[p, half, side]) + to_k[s][:, side]).astype(BF16),
                (tn(ws[p, s, i], gs[p, half, side]) + to_v[s][:, side]).astype(BF16),
            ))
        for (s, i), values in zip(PLACES, made):
            for ref, value in zip((gq, gk, gv), values):
                ref[HALVES[s], pl.ds(pl.multiple_of(p * PAIR + i * DH, DH), DH)] = value

    def gcopy(o):
        return pltpu.make_async_remote_copy(
            src_ref=gslots.at[rank], dst_ref=gslots.at[rank], send_sem=gsend.at[o], recv_sem=grecv.at[rank],
            device_id=device(lax.rem(rank + o, n)), device_id_type=MESH,
        )

    def share_gain(p):
        for o in range(1, n):
            gcopy(o).start()

    steps = max(len(order) for order in orders)
    words = []
    for at in range(0, steps, SLOTS):
        word = jnp.int32(0)
        for c, order in enumerate(orders):
            codes = [UNITS.index(u) + (p << 4) for u, p in order[at:at + SLOTS]]
            codes += [15] * (SLOTS - len(codes))
            bits = sum(code << (7 * j) for j, code in enumerate(codes))
            word = jnp.where(chip == c, jnp.int32(bits), word)
        words.append(word)
    held = min(4, pairs)

    def unit_at(i):
        group = lax.div(i, SLOTS)
        word = words[0]
        for g in range(1, len(words)):
            word = jnp.where(group == g, words[g], word)
        code = lax.shift_right_logical(word, 7 * lax.rem(i, SLOTS)) & 127
        return code & 15, lax.shift_right_logical(code, 4)

    def local_and_send(i, p):
        local(p)

        @pl.when(i == held - 1)
        def _():
            pl.semaphore_wait(barrier, n - 1)
            for j in range(held):
                ahead.to_partner(unit_at(j)[1]).start()

        @pl.when(i >= held)
        def _():
            ahead.to_partner(p).start()

    def one(fn):
        return lambda i, p: fn(p)

    work = (local_and_send,) + tuple(
        one(fn) for fn in (
            scores, ahead.step, forward, back.step, grads, share_gain, ahead.early, ahead.rest, back.early, back.rest,
        )
    )
    if not split_f + split_b:
        work = work[:7]

    def step(i, c):
        unit, p = unit_at(i)
        for u, fn in enumerate(work):
            pl.when(unit == u)(functools.partial(fn, i, p))
        return c

    lax.fori_loop(0, steps, step, 0)

    for o in range(1, n):
        src = lax.rem(rank + n - o, n)
        pltpu.make_async_remote_copy(
            src_ref=gslots.at[src], dst_ref=gslots.at[src], send_sem=gsend.at[o], recv_sem=grecv.at[src],
            device_id=device(src), device_id_type=MESH,
        ).wait_recv()
        gcopy(o).wait_send()
    summed = gslots[0]
    for i in range(1, n):
        summed = summed + gslots[i]
    ggain[...] = summed * (1.0 / math.sqrt(total))

    def finish(p):
        ahead.finish(p)
        back.finish(p)

    each(finish)


def writer(*refs):
    count = len(refs) // 2
    sems = refs[-1]
    copies = [pltpu.make_async_copy(refs[i], refs[count + i], sems.at[i]) for i in range(count)]
    for copy in copies:
        copy.start()
    for copy in copies:
        copy.wait()


def shards(queries, keys, values, d_out, doc_lengths, gain):
    tokens, width = queries.shape
    pairs = width // PAIR
    heads = 2 * pairs
    seqs, reps = lax.axis_size("seq"), lax.axis_size("rep")
    n = seqs * reps
    slab = pltpu.VMEM((pairs, tokens, PAIR), BF16)
    rows = pltpu.VMEM((tokens, PAIR), BF16)
    state = pltpu.VMEM((heads, DH, DH), F32)
    half = pltpu.VMEM((pairs, DH, DH), F32)
    dma = pltpu.SemaphoreType.DMA
    big = jax.ShapeDtypeStruct((tokens, width), BF16)
    hbm = pl.BlockSpec(memory_space=pltpu.HBM)
    in_hbm = functools.partial(pltpu.with_memory_space_constraint, memory_space=pltpu.HBM)
    vmem = pl.BlockSpec(memory_space=pltpu.VMEM)
    shapes = (big, big, big, big, jax.ShapeDtypeStruct((heads, DH), F32))
    out = pl.pallas_call(
        functools.partial(kernel, pairs, tokens, seqs, reps, doc_lengths.shape[0]),
        out_shape=shapes,
        in_specs=[hbm] * 6,
        out_specs=(vmem,) * 5,
        scratch_shapes=[
            pltpu.SMEM(doc_lengths.shape, jnp.int32),
            pltpu.VMEM((heads, DH), F32),
            slab, slab, slab, slab,
            pltpu.VMEM((pairs, tokens, PAIR), F32),
            pltpu.VMEM((pairs, 2, 2, HALF, HALF), BF16),
            slab,
            pltpu.VMEM((2, HALF, HALF), F32),
            rows, rows, rows, rows,
            state, state, half, half, half, half, half, half, state,
            state, state, half, half, half, half, half, half, state,
            pltpu.VMEM((pairs, 2, PAIR, PAIR), BF16),
            pltpu.VMEM((2, PAIR, PAIR), BF16),
            pltpu.VMEM((n, heads, DH), F32),
            dma((4, pairs)), dma((2,)), dma((4, 2, pairs)), dma((4, 2, pairs)),
            dma((n,)), dma((n,)),
        ],
        compiler_params=pltpu.CompilerParams(
            collective_id=0, has_side_effects=True, vmem_limit_bytes=44 << 20
        ),
    )(in_hbm(doc_lengths), in_hbm(gain.reshape(heads, DH)), queries, keys, values, d_out)
    out = pl.pallas_call(
        writer,
        out_shape=shapes,
        in_specs=[pl.BlockSpec(memory_space=pl.ANY)] * 5,
        out_specs=(hbm,) * 5,
        scratch_shapes=[dma((5,))],
        compiler_params=pltpu.CompilerParams(vmem_limit_bytes=1 << 20),
    )(*out)
    return (*out[:4], out[4].reshape(1, width))


def solution(mesh):
    token = P(("groups", "seq", "rep"), "head")
    return jax.shard_map(
        shards,
        mesh=mesh,
        in_specs=(token, token, token, token, P("groups"), P("head")),
        out_specs=(token, token, token, token, P("groups", "head")),
        check_vma=False,
    )
```

```python
import functools
import math

import jax
import jax.numpy as jnp
from jax import lax
from jax.experimental import pallas as pl
from jax.experimental.pallas import tpu as pltpu
from jax.sharding import PartitionSpec as P

DH = 128
PAIR = 2 * DH
HALF = 256
MESH = pl.DeviceIdType.MESH
F32 = jnp.float32
BF16 = jnp.bfloat16
TOP, BOT = slice(0, HALF), slice(HALF, 2 * HALF)
HALVES = (TOP, BOT)
SIDES = (slice(0, DH), slice(DH, PAIR))

UNITS = "ABFCKDGEHLM"
PLANS = {
    (4, 8): (
        (1, 4, 6, 7),
        (0, 2, 3, 5),
        (
            (
                "A0A1A2A5B0B1F0F5F2B5B2H1A4B4A3B3H4A6B6F3A7B7H6C1H7C5C0C2C4C3",
                "C6C7M0D0M5D5M2D2K1G0D1K4M3D4D3K6K7D6D7",
            ),
            (
                "A0A1A4A6B0B1E1E6E4B6B4A5B5A3B3A7B7F0A2B2E7C0F5F2C5C2H1H4C1F3",
                "C4C3H6H7L0C6C7L5L2K1G0D1K4L3D4K6D6K7M0D7M5D0M2D5M3D2D3",
            ),
            (
                "A0A1A4A6A7A5A3A2B1B6B7B4B5B0B3B2E1E6E4F0C0E7F5L0C5F2H1L5C2H4",
                "C1L2F3C4K1H6C3K4H7C6L3C7G0K6D1K7D6M0D7M5D4M2D5D0M3D2D3",
            ),
            (
                "A0A1A2A4A3A7A6A5B0B1B2B4B3B7B6B5H1C1H6H4K1C6F0C4K6C0K4H7F5D1",
                "C7F2C5K7C2M0M5F3D4M2C3G0D0D2M3D7D6D3D5",
            ),
        ),
    ),
}
SLOTS = 4


def plan_of(seqs, pairs):
    every = range(pairs)
    plain = [("A", p) for p in every] + [("B", p) for p in every] + [(u, p) for p in every for u in "FC"]
    plain += [("K", 0), ("G", 0), ("D", 0)] + [(u, p) for p in every[1:] for u in "KD"]
    if (seqs, pairs) not in PLANS:
        return (), (), (plain,) * seqs
    ahead, back, orders = PLANS[seqs, pairs]
    texts = ["".join(parts) for parts in orders]
    return ahead, back, [[(t[i], int(t[i + 1])) for i in range(0, len(t), 2)] for t in texts]


def nn(a, b):
    return lax.dot_general(a, b, (((1,), (0,)), ((), ())), preferred_element_type=F32)


def nt(a, b):
    return lax.dot_general(a, b, (((1,), (1,)), ((), ())), preferred_element_type=F32)


def tn(a, b):
    return lax.dot_general(a, b, (((0,), (0,)), ((), ())), preferred_element_type=F32)


def kernel(
    pairs, tokens, seqs, reps, ndoc,
    lens_hbm, gain_hbm, q_hbm, k_hbm, v_hbm, d_hbm,
    mix, gq, gk, gv, ggain,
    lens, gain, qs, ks, vs, ds, acc, ws, gs, mask, fwd_m, bwd_m, tail_m, head_m,
    fown, fhalf, fpart, fin, fin2, fout, fout2, frel, fstate,
    bown, bhalf, bpart, bin_, bin2, bout, bout2, brel, bstate,
    sb, gsb, gslots,
    in_sem, small_sem, fsem, bsem, gsend, grecv,
):
    n = seqs * reps
    chip, core = lax.axis_index("seq"), lax.axis_index("rep")
    rank = chip * reps + core
    total = n * tokens
    first = rank * tokens
    middle = first + HALF

    def device(other):
        return {"seq": lax.div(other, reps), "rep": lax.rem(other, reps)}

    def cols(p):
        return pl.ds(pl.multiple_of(p * PAIR, PAIR), PAIR)

    def load(i, hbm, buf, p):
        return pltpu.make_async_copy(hbm.at[:, cols(p)], buf.at[p], in_sem.at[i, p])

    def each(fn):
        lax.fori_loop(0, pairs, lambda p, c: (fn(p), c)[1], 0)

    def start_kv(p):
        load(0, k_hbm, ks, p).start()
        load(1, v_hbm, vs, p).start()

    def start_qd(p):
        load(2, q_hbm, qs, p).start()
        load(3, d_hbm, ds, p).start()

    lens_copy = pltpu.make_async_copy(lens_hbm, lens, small_sem.at[0])
    gain_copy = pltpu.make_async_copy(gain_hbm, gain, small_sem.at[1])
    lens_copy.start()
    gain_copy.start()
    each(start_kv)
    each(start_qd)
    barrier = pltpu.get_barrier_semaphore()
    other_core = {"rep": 1 - core}
    chip_on, chip_back = {"seq": jnp.minimum(chip + 1, seqs - 1)}, {"seq": jnp.maximum(chip - 1, 0)}
    pl.semaphore_signal(barrier, inc=1, device_id=other_core, device_id_type=MESH)

    @pl.when(chip < seqs - 1)
    def _():
        pl.semaphore_signal(barrier, inc=1, device_id=chip_on, device_id_type=MESH)

    @pl.when(chip > 0)
    def _():
        pl.semaphore_signal(barrier, inc=1, device_id=chip_back, device_id_type=MESH)

    lens_copy.wait()
    gain_copy.wait()

    ends = []
    run = jnp.int32(0)
    for i in range(ndoc):
        run = run + lens[i]
        ends.append(run)

    def doc_of(place):
        return sum((jnp.where(e <= place, 1, 0) for e in ends))

    before, after = doc_of(first - 1), doc_of(first + tokens)
    doc_first, doc_last = doc_of(first), doc_of(first + tokens - 1)
    doc_up, doc_down = doc_of(middle - 1), doc_of(middle)
    col = lax.broadcasted_iota(jnp.int32, (HALF, DH), 0)
    place_row = lax.broadcasted_iota(jnp.int32, (8, HALF), 1)

    def spread(ref, s, hit):
        ones = jnp.where(hit, 1.0, 0.0).astype(BF16)
        for side in SIDES:
            ref[HALVES[s], side] = ones

    for s in range(2):
        doc_col = doc_of(col + (first + s * HALF))
        spread(fwd_m, s, doc_col == (doc_up if s else before))
        spread(bwd_m, s, doc_col == (after if s else doc_down))
        spread(tail_m, s, doc_col == (doc_last if s else doc_up))
        spread(head_m, s, doc_col == (doc_down if s else doc_first))
        doc_row = doc_of(place_row + (first + s * HALF))
        for side in SIDES:
            keep = (doc_col == doc_row[0:1, side]) & (col >= place_row[0:1, side])
            mask[s, :, side] = jnp.where(keep, 1.0 / DH, 0.0)

    def same(one, other):
        return jnp.where(one == other, 1.0, 0.0)

    def carries(one, other):
        return same(doc_of(one), doc_of(other))

    up_last, up_before = same(doc_up, doc_last), same(doc_up, before)
    down_first, down_after = same(doc_down, doc_first), same(doc_down, after)

    base = chip * reps * tokens
    flags_f = [carries(base + i * tokens - 1, base + (i + 1) * tokens - 1) for i in range(2)]
    flags_b = [carries(base + i * tokens, base + (i + 1) * tokens) for i in (1, 0)]

    @pl.when(chip == 0)
    def _():
        fin[...] = jnp.zeros_like(fin)

    @pl.when(chip == seqs - 1)
    def _():
        bin_[...] = jnp.zeros_like(bin_)

    split_f, split_b, orders = plan_of(seqs, pairs)

    for split, place, later in ((split_f, chip, fin2), (split_b, seqs - 1 - chip, bin2)):
        if split:
            @pl.when(place != 2)
            def _():
                later[...] = jnp.zeros_like(later)

    def clear(p):
        for s in range(2):
            for i in range(2):
                sb[p, s, SIDES[i], SIDES[1 - i]] = jnp.zeros((DH, DH), BF16)

    each(clear)
    for s in range(2):
        for i in range(2):
            gsb[s, SIDES[i], SIDES[1 - i]] = jnp.zeros((DH, DH), BF16)

    class Chain:
        def __init__(self, own, part, arrived, arrived2, out, out2, rel, state, sems, late, flags, place, onward, split):
            self.own, self.part, self.arrived, self.arrived2 = own, part, arrived, arrived2
            self.out, self.out2, self.rel, self.state, self.sems = out, out2, rel, state, sems
            f0, f1 = flags
            self.c_own, self.c_part = jnp.where(late, 1.0, f1), jnp.where(late, f1, 1.0)
            self.c_in = f0 * f1
            self.own_part, self.own_in = jnp.where(late, 1.0, 0.0), jnp.where(late, f0, 1.0)
            self.rel_own, self.rel_in = jnp.where(late, 0.0, 1.0), jnp.where(late, 1.0, f0)
            self.place, self.onward = place, onward
            self.is_first, self.is_last = place == 0, place == seqs - 1
            self.split = sum(1 << p for p in split)

        def remote(self, src, dst, kind, p, where):
            return pltpu.make_async_remote_copy(
                src_ref=src, dst_ref=dst, send_sem=self.sems.at[kind, 0, p], recv_sem=self.sems.at[kind, 1, p],
                device_id=where, device_id_type=MESH,
            )

        def to_partner(self, p):
            return self.remote(self.own.at[2 * p + 1 - core], self.part.at[p], 0, p, other_core)

        def to_next(self, p):
            return self.remote(self.out.at[p], self.arrived.at[p], 1, p, self.onward)

        def relay(self, p):
            return self.remote(self.rel.at[p], self.state.at[2 * p + core], 2, p, other_core)

        def after(self, p):
            return self.remote(self.out2.at[p], self.arrived2.at[p], 3, p, self.onward)

        def keep(self, p, own, part, came):
            self.rel[p] = self.rel_own * own + self.rel_in * came
            self.relay(p).start()
            self.state[2 * p + core] = self.own_part * part + self.own_in * came

        def step(self, p):
            self.to_partner(p).wait_recv()

            @pl.when(jnp.logical_not(self.is_first))
            def _():
                self.to_next(p).wait_recv()

            own, part, came = self.own[2 * p + core], self.part[p], self.arrived[p]

            @pl.when(jnp.logical_not(self.is_last))
            def _():
                self.out[p] = self.c_own * own + self.c_part * part + self.c_in * came
                self.to_next(p).start()

            self.keep(p, own, part, came)

        def early(self, p):
            self.to_partner(p).wait_recv()
            both = self.c_own * self.own[2 * p + core] + self.c_part * self.part[p]

            @pl.when(self.place == 1)
            def _():
                self.out[p] = both

            @pl.when(self.place == 2)
            def _():
                self.to_next(p).wait_recv()
                self.out[p] = both + self.c_in * self.arrived[p]

            self.to_next(p).start()

        def rest(self, p):
            @pl.when(self.is_first | self.is_last)
            def _():
                self.to_partner(p).wait_recv()

            @pl.when((self.place == 1) | self.is_last)
            def _():
                self.to_next(p).wait_recv()

            @pl.when(self.is_first)
            def _():
                self.out[p] = self.c_own * self.own[2 * p + core] + self.c_part * self.part[p]
                self.to_next(p).start()

            @pl.when(self.place == 1)
            def _():
                self.out2[p] = self.c_in * self.arrived[p]
                self.after(p).start()

            @pl.when(self.place == 2)
            def _():
                self.after(p).wait_recv()

            self.keep(p, self.own[2 * p + core], self.part[p], self.arrived[p] + self.arrived2[p])

        def take(self, p):
            self.remote(self.rel.at[p], self.state.at[2 * p + 1 - core], 2, p, other_core).wait_recv()

        def finish(self, p):
            self.to_partner(p).wait_send()
            self.relay(p).wait_send()

            @pl.when(jnp.logical_not(self.is_last))
            def _():
                self.to_next(p).wait_send()

            if self.split:
                other_way = lax.shift_right_logical(jnp.int32(self.split), p) & 1

                @pl.when((self.place == 1) & (other_way == 1))
                def _():
                    self.after(p).wait_send()

    ahead = Chain(
        fown, fpart, fin, fin2, fout, fout2, frel, fstate, fsem, core == 1, flags_f,
        chip, chip_on, split_f,
    )
    back = Chain(
        bown, bpart, bin_, bin2, bout, bout2, brel, bstate, bsem, core == 0, flags_b,
        seqs - 1 - chip, chip_back, split_b,
    )

    def local(p):
        load(0, k_hbm, ks, p).wait()
        load(1, v_hbm, vs, p).wait()
        sums = [tn(ks[p, s] * tail_m[s], vs[p, s]) for s in HALVES]
        for i, side in enumerate(SIDES):
            up, low = (x[side, side] for x in sums)
            fhalf[2 * p + i] = up
            fown[2 * p + i] = low + up_last * up

    PLACES = [(s, i) for s in range(2) for i in range(2)]

    def scores(p):
        load(2, q_hbm, qs, p).wait()
        raw = [nt(qs[p, HALVES[s], SIDES[i]], ks[p, HALVES[s], SIDES[i]]) for s, i in PLACES]
        kept = [(x * mask[s]).astype(BF16) for x, (s, i) in zip(raw, PLACES)]
        sums = [nn(w, vs[p, HALVES[s], SIDES[i]]) for w, (s, i) in zip(kept, PLACES)]
        for w, x, (s, i) in zip(kept, sums, PLACES):
            ws[p, s, i] = w
            acc[p, HALVES[s], SIDES[i]] = x

    def forward(p):
        ahead.take(p)
        load(3, d_hbm, ds, p).wait()
        for i, side in enumerate(SIDES):
            state = fstate[2 * p + i]
            sb[p, 0, side, side] = (state * (1.0 / DH)).astype(BF16)
            sb[p, 1, side, side] = ((up_before * state + fhalf[2 * p + i]) * (1.0 / DH)).astype(BF16)
        carried = [nn(qs[p, HALVES[s]] * fwd_m[HALVES[s]], sb[p, s]) for s in range(2)]
        gains = [gain[pl.ds(2 * p + i, 1), :] for i in range(2)]
        made = []
        for s, i in PLACES:
            half, side = HALVES[s], SIDES[i]
            attn = acc[p, half, side] + carried[s][:, side]
            inverse = lax.rsqrt(jnp.mean(attn * attn, axis=-1, keepdims=True) + 1e-5)
            normed = attn * inverse
            mixed = (normed * gains[i]).astype(BF16)
            d = ds[p, half, side].astype(F32)
            terms = jnp.sum(d * normed, axis=0, keepdims=True)
            g = d * gains[i]
            inner = jnp.mean(g * normed, axis=-1, keepdims=True)
            made.append((mixed, (inverse * (g - normed * inner)).astype(BF16), terms))
        for (s, i), (mixed, grad, terms) in zip(PLACES, made):
            mix[HALVES[s], pl.ds(pl.multiple_of(p * PAIR + i * DH, DH), DH)] = mixed
            gs[p, HALVES[s], SIDES[i]] = grad
        for i, side in enumerate(SIDES):
            gslots[rank, pl.ds(2 * p + i, 1), :] = made[i][2] + made[2 + i][2]
        sums = [tn(qs[p, s] * head_m[s], gs[p, s]) for s in HALVES]
        for i, side in enumerate(SIDES):
            up, low = (x[side, side] for x in sums)
            bhalf[2 * p + i] = low
            bown[2 * p + i] = up + down_first * low
        back.to_partner(p).start()

    def grads(p):
        back.take(p)
        for i, side in enumerate(SIDES):
            state = bstate[2 * p + i]
            gsb[1, side, side] = (state * (1.0 / DH)).astype(BF16)
            gsb[0, side, side] = ((down_after * state + bhalf[2 * p + i]) * (1.0 / DH)).astype(BF16)
        raw = [nt(gs[p, HALVES[s], SIDES[i]], vs[p, HALVES[s], SIDES[i]]) for s, i in PLACES]
        kept = [(x * mask[s]).astype(BF16) for x, (s, i) in zip(raw, PLACES)]
        to_q = [nt(gs[p, HALVES[s]] * fwd_m[HALVES[s]], sb[p, s]) for s in range(2)]
        to_k = [nt(vs[p, HALVES[s]] * bwd_m[HALVES[s]], gsb[s]) for s in range(2)]
        to_v = [nn(ks[p, HALVES[s]] * bwd_m[HALVES[s]], gsb[s]) for s in range(2)]
        made = []
        for g, (s, i) in zip(kept, PLACES):
            half, side = HALVES[s], SIDES[i]
            made.append((
                (nn(g, ks[p, half, side]) + to_q[s][:, side]).astype(BF16),
                (tn(g, qs[p, half, side]) + to_k[s][:, side]).astype(BF16),
                (tn(ws[p, s, i], gs[p, half, side]) + to_v[s][:, side]).astype(BF16),
            ))
        for (s, i), values in zip(PLACES, made):
            for ref, value in zip((gq, gk, gv), values):
                ref[HALVES[s], pl.ds(pl.multiple_of(p * PAIR + i * DH, DH), DH)] = value

    def gcopy(o):
        return pltpu.make_async_remote_copy(
            src_ref=gslots.at[rank], dst_ref=gslots.at[rank], send_sem=gsend.at[o], recv_sem=grecv.at[rank],
            device_id=device(lax.rem(rank + o, n)), device_id_type=MESH,
        )

    def share_gain(p):
        for o in range(1, n):
            gcopy(o).start()

    steps = max(len(order) for order in orders)
    words = []
    for at in range(0, steps, SLOTS):
        word = jnp.int32(0)
        for c, order in enumerate(orders):
            codes = [UNITS.index(u) + (p << 4) for u, p in order[at:at + SLOTS]]
            codes += [15] * (SLOTS - len(codes))
            bits = sum(code << (7 * j) for j, code in enumerate(codes))
            word = jnp.where(chip == c, jnp.int32(bits), word)
        words.append(word)
    held = min(4, pairs)

    def unit_at(i):
        group = lax.div(i, SLOTS)
        word = words[0]
        for g in range(1, len(words)):
            word = jnp.where(group == g, words[g], word)
        code = lax.shift_right_logical(word, 7 * lax.rem(i, SLOTS)) & 127
        return code & 15, lax.shift_right_logical(code, 4)

    def local_and_send(i, p):
        local(p)

        @pl.when(i == held - 1)
        def _():
            inner = (chip > 0) & (chip < seqs - 1)

            @pl.when(inner)
            def _():
                pl.semaphore_wait(barrier, 3)

            @pl.when(jnp.logical_not(inner))
            def _():
                pl.semaphore_wait(barrier, 2)

            for j in range(held):
                ahead.to_partner(unit_at(j)[1]).start()

        @pl.when(i >= held)
        def _():
            ahead.to_partner(p).start()

    def one(fn):
        return lambda i, p: fn(p)

    work = (local_and_send,) + tuple(
        one(fn) for fn in (
            scores, ahead.step, forward, back.step, grads, share_gain, ahead.early, ahead.rest, back.early, back.rest,
        )
    )
    if not split_f + split_b:
        work = work[:7]

    def step(i, c):
        unit, p = unit_at(i)
        for u, fn in enumerate(work):
            pl.when(unit == u)(functools.partial(fn, i, p))
        return c

    lax.fori_loop(0, steps, step, 0)

    for o in range(1, n):
        src = lax.rem(rank + n - o, n)
        pltpu.make_async_remote_copy(
            src_ref=gslots.at[src], dst_ref=gslots.at[src], send_sem=gsend.at[o], recv_sem=grecv.at[src],
            device_id=device(src), device_id_type=MESH,
        ).wait_recv()
        gcopy(o).wait_send()
    summed = gslots[0]
    for i in range(1, n):
        summed = summed + gslots[i]
    ggain[...] = summed * (1.0 / math.sqrt(total))

    def finish(p):
        ahead.finish(p)
        back.finish(p)

    each(finish)


def writer(*refs):
    count = len(refs) // 2
    sems = refs[-1]
    copies = [pltpu.make_async_copy(refs[i], refs[count + i], sems.at[i]) for i in range(count)]
    for copy in copies:
        copy.start()
    for copy in copies:
        copy.wait()


def shards(queries, keys, values, d_out, doc_lengths, gain):
    tokens, width = queries.shape
    pairs = width // PAIR
    heads = 2 * pairs
    seqs, reps = lax.axis_size("seq"), lax.axis_size("rep")
    n = seqs * reps
    slab = pltpu.VMEM((pairs, tokens, PAIR), BF16)
    rows = pltpu.VMEM((tokens, PAIR), BF16)
    state = pltpu.VMEM((heads, DH, DH), F32)
    half = pltpu.VMEM((pairs, DH, DH), F32)
    dma = pltpu.SemaphoreType.DMA
    big = jax.ShapeDtypeStruct((tokens, width), BF16)
    hbm = pl.BlockSpec(memory_space=pltpu.HBM)
    in_hbm = functools.partial(pltpu.with_memory_space_constraint, memory_space=pltpu.HBM)
    vmem = pl.BlockSpec(memory_space=pltpu.VMEM)
    shapes = (big, big, big, big, jax.ShapeDtypeStruct((heads, DH), F32))
    out = pl.pallas_call(
        functools.partial(kernel, pairs, tokens, seqs, reps, doc_lengths.shape[0]),
        out_shape=shapes,
        in_specs=[hbm] * 6,
        out_specs=(vmem,) * 5,
        scratch_shapes=[
            pltpu.SMEM(doc_lengths.shape, jnp.int32),
            pltpu.VMEM((heads, DH), F32),
            slab, slab, slab, slab,
            pltpu.VMEM((pairs, tokens, PAIR), F32),
            pltpu.VMEM((pairs, 2, 2, HALF, HALF), BF16),
            slab,
            pltpu.VMEM((2, HALF, HALF), F32),
            rows, rows, rows, rows,
            state, state, half, half, half, half, half, half, state,
            state, state, half, half, half, half, half, half, state,
            pltpu.VMEM((pairs, 2, PAIR, PAIR), BF16),
            pltpu.VMEM((2, PAIR, PAIR), BF16),
            pltpu.VMEM((n, heads, DH), F32),
            dma((4, pairs)), dma((2,)), dma((4, 2, pairs)), dma((4, 2, pairs)),
            dma((n,)), dma((n,)),
        ],
        compiler_params=pltpu.CompilerParams(
            collective_id=0, has_side_effects=True, vmem_limit_bytes=44 << 20
        ),
    )(in_hbm(doc_lengths), in_hbm(gain.reshape(heads, DH)), queries, keys, values, d_out)
    out = pl.pallas_call(
        writer,
        out_shape=shapes,
        in_specs=[pl.BlockSpec(memory_space=pl.ANY)] * 5,
        out_specs=(hbm,) * 5,
        scratch_shapes=[dma((5,))],
        compiler_params=pltpu.CompilerParams(vmem_limit_bytes=1 << 20),
    )(*out)
    return (*out[:4], out[4].reshape(1, width))


def solution(mesh):
    token = P(("groups", "seq", "rep"), "head")
    return jax.shard_map(
        shards,
        mesh=mesh,
        in_specs=(token, token, token, token, P("groups"), P("head")),
        out_specs=(token, token, token, token, P("groups", "head")),
        check_vma=False,
    )
```

```python
import functools
import math

import jax
import jax.numpy as jnp
from jax import lax
from jax.experimental import pallas as pl
from jax.experimental.pallas import tpu as pltpu
from jax.sharding import PartitionSpec as P

DH = 128
PAIR = 2 * DH
HALF = 256
MESH = pl.DeviceIdType.MESH
F32 = jnp.float32
BF16 = jnp.bfloat16
TOP, BOT = slice(0, HALF), slice(HALF, 2 * HALF)
HALVES = (TOP, BOT)
SIDES = (slice(0, DH), slice(DH, PAIR))

UNITS = "ABFCKDGEHLM"
PLANS = {
    (4, 8): (
        (1, 4, 6, 7),
        (0, 2, 3, 5),
        (
            (
                "A0A1A2A5B0B1F0F5F2B5B2H1A4B4A3B3H4A6B6F3A7B7H6C1H7C5C0C2C4C3",
                "C6C7M0D0M5D5M2D2K1G0D1K4M3D4D3K6K7D6D7",
            ),
            (
                "A0A1A4A6B0B1E1E6E4B6B4A5B5A3B3A7B7F0A2B2E7C0F5F2C5C2H1H4C1F3",
                "C4C3H6H7L0C6C7L5L2K1G0D1K4L3D4K6D6K7M0D7M5D0M2D5M3D2D3",
            ),
            (
                "A0A1A4A6A7A5A3A2B1B6B7B4B5B0B3B2E1E6E4F0C0E7F5L0C5F2H1L5C2H4",
                "C1L2F3C4K1H6C3K4H7C6L3C7G0K6D1K7D6M0D7M5D4M2D5D0M3D2D3",
            ),
            (
                "A0A1A2A4A3A7A6A5B0B1B2B4B3B7B6B5H1C1H6H4K1C6F0C4K6C0K4H7F5D1",
                "C7F2C5K7C2M0M5F3D4M2C3G0D0D2M3D7D6D3D5",
            ),
        ),
    ),
}
SLOTS = 4
TAIL = 2


def plan_of(seqs, pairs):
    every = range(pairs)
    plain = [("A", p) for p in every] + [("B", p) for p in every] + [(u, p) for p in every for u in "FC"]
    plain += [("K", 0), ("G", 0), ("D", 0)] + [(u, p) for p in every[1:] for u in "KD"]
    if (seqs, pairs) not in PLANS:
        return (), (), (plain,) * seqs
    ahead, back, orders = PLANS[seqs, pairs]
    texts = ["".join(parts) for parts in orders]
    return ahead, back, [[(t[i], int(t[i + 1])) for i in range(0, len(t), 2)] for t in texts]


def tail_lists(seqs, pairs):
    kept = min(TAIL, pairs)
    return [[p for u, p in order if u == "D"][pairs - kept:] for order in plan_of(seqs, pairs)[2]]


def tails_of(seqs, pairs, chip):
    lists = tail_lists(seqs, pairs)
    picked = []
    for j in range(len(lists[0])):
        pair = jnp.int32(lists[0][j])
        for c in range(1, seqs):
            pair = jnp.where(chip == c, jnp.int32(lists[c][j]), pair)
        picked.append(pair)
    return picked


def nn(a, b):
    return lax.dot_general(a, b, (((1,), (0,)), ((), ())), preferred_element_type=F32)


def nt(a, b):
    return lax.dot_general(a, b, (((1,), (1,)), ((), ())), preferred_element_type=F32)


def tn(a, b):
    return lax.dot_general(a, b, (((0,), (0,)), ((), ())), preferred_element_type=F32)


PLACES = [(s, i) for s in range(2) for i in range(2)]


def pair_columns(p, i=0, width=PAIR):
    return pl.ds(pl.multiple_of(p * PAIR + i * DH, DH), width)


def input_grads(p, qs, ks, vs, gs, ws, sb, low, mask, fwd_m, bwd_m):
    raw = [nt(gs[p, HALVES[s], SIDES[i]], vs[p, HALVES[s], SIDES[i]]) for s, i in PLACES]
    kept = [(x * mask[s]).astype(BF16) for x, (s, i) in zip(raw, PLACES)]
    to_q = [nt(gs[p, HALVES[s]] * fwd_m[HALVES[s]], sb[p, s]) for s in range(2)]
    to_k = [nt(vs[p, HALVES[s]] * bwd_m[HALVES[s]], low[s]) for s in range(2)]
    to_v = [nn(ks[p, HALVES[s]] * bwd_m[HALVES[s]], low[s]) for s in range(2)]
    made = []
    for g, (s, i) in zip(kept, PLACES):
        half, side = HALVES[s], SIDES[i]
        made.append((
            (nn(g, ks[p, half, side]) + to_q[s][:, side]).astype(BF16),
            (tn(g, qs[p, half, side]) + to_k[s][:, side]).astype(BF16),
            (tn(ws[p, s, i], gs[p, half, side]) + to_v[s][:, side]).astype(BF16),
        ))
    return made


def kernel(
    pairs, tokens, seqs, reps, ndoc,
    lens_hbm, gain_hbm, q_hbm, k_hbm, v_hbm, d_hbm,
    mix, gq, gk, gv, ggain, qs, ks, vs, gs, ws, sb, gsb_tail, mask, fwd_m, bwd_m,
    lens, gain, ds, acc, tail_m, head_m,
    fown, fhalf, fpart, fin, fin2, fout, fout2, frel, fstate,
    bown, bhalf, bpart, bin_, bin2, bout, bout2, brel, bstate,
    gsb, gslots,
    in_sem, small_sem, fsem, bsem, gsend, grecv,
):
    n = seqs * reps
    chip, core = lax.axis_index("seq"), lax.axis_index("rep")
    rank = chip * reps + core
    total = n * tokens
    first = rank * tokens
    middle = first + HALF

    def device(other):
        return {"seq": lax.div(other, reps), "rep": lax.rem(other, reps)}

    def cols(p):
        return pl.ds(pl.multiple_of(p * PAIR, PAIR), PAIR)

    def load(i, hbm, buf, p):
        return pltpu.make_async_copy(hbm.at[:, cols(p)], buf.at[p], in_sem.at[i, p])

    def each(fn):
        lax.fori_loop(0, pairs, lambda p, c: (fn(p), c)[1], 0)

    def start_kv(p):
        load(0, k_hbm, ks, p).start()
        load(1, v_hbm, vs, p).start()

    def start_qd(p):
        load(2, q_hbm, qs, p).start()
        load(3, d_hbm, ds, p).start()

    lens_copy = pltpu.make_async_copy(lens_hbm, lens, small_sem.at[0])
    gain_copy = pltpu.make_async_copy(gain_hbm, gain, small_sem.at[1])
    lens_copy.start()
    gain_copy.start()
    each(start_kv)
    each(start_qd)
    barrier = pltpu.get_barrier_semaphore()
    other_core = {"rep": 1 - core}
    chip_on, chip_back = {"seq": jnp.minimum(chip + 1, seqs - 1)}, {"seq": jnp.maximum(chip - 1, 0)}
    pl.semaphore_signal(barrier, inc=1, device_id=other_core, device_id_type=MESH)

    @pl.when(chip < seqs - 1)
    def _():
        pl.semaphore_signal(barrier, inc=1, device_id=chip_on, device_id_type=MESH)

    @pl.when(chip > 0)
    def _():
        pl.semaphore_signal(barrier, inc=1, device_id=chip_back, device_id_type=MESH)

    lens_copy.wait()
    gain_copy.wait()

    ends = []
    run = jnp.int32(0)
    for i in range(ndoc):
        run = run + lens[i]
        ends.append(run)

    def doc_of(place):
        return sum((jnp.where(e <= place, 1, 0) for e in ends))

    before, after = doc_of(first - 1), doc_of(first + tokens)
    doc_first, doc_last = doc_of(first), doc_of(first + tokens - 1)
    doc_up, doc_down = doc_of(middle - 1), doc_of(middle)
    col = lax.broadcasted_iota(jnp.int32, (HALF, DH), 0)
    place_row = lax.broadcasted_iota(jnp.int32, (8, HALF), 1)

    def spread(ref, s, hit):
        ones = jnp.where(hit, 1.0, 0.0).astype(BF16)
        for side in SIDES:
            ref[HALVES[s], side] = ones

    for s in range(2):
        doc_col = doc_of(col + (first + s * HALF))
        spread(fwd_m, s, doc_col == (doc_up if s else before))
        spread(bwd_m, s, doc_col == (after if s else doc_down))
        spread(tail_m, s, doc_col == (doc_last if s else doc_up))
        spread(head_m, s, doc_col == (doc_down if s else doc_first))
        doc_row = doc_of(place_row + (first + s * HALF))
        for side in SIDES:
            keep = (doc_col == doc_row[0:1, side]) & (col >= place_row[0:1, side])
            mask[s, :, side] = jnp.where(keep, 1.0 / DH, 0.0)

    def same(one, other):
        return jnp.where(one == other, 1.0, 0.0)

    def carries(one, other):
        return same(doc_of(one), doc_of(other))

    up_last, up_before = same(doc_up, doc_last), same(doc_up, before)
    down_first, down_after = same(doc_down, doc_first), same(doc_down, after)

    base = chip * reps * tokens
    flags_f = [carries(base + i * tokens - 1, base + (i + 1) * tokens - 1) for i in range(2)]
    flags_b = [carries(base + i * tokens, base + (i + 1) * tokens) for i in (1, 0)]

    @pl.when(chip == 0)
    def _():
        fin[...] = jnp.zeros_like(fin)

    @pl.when(chip == seqs - 1)
    def _():
        bin_[...] = jnp.zeros_like(bin_)

    split_f, split_b, orders = plan_of(seqs, pairs)

    for split, place, later in ((split_f, chip, fin2), (split_b, seqs - 1 - chip, bin2)):
        if split:
            @pl.when(place != 2)
            def _():
                later[...] = jnp.zeros_like(later)

    def clear(p):
        for s in range(2):
            for i in range(2):
                sb[p, s, SIDES[i], SIDES[1 - i]] = jnp.zeros((DH, DH), BF16)

    each(clear)
    tails = tails_of(seqs, pairs, chip)
    for s in range(2):
        for i in range(2):
            gsb[s, SIDES[i], SIDES[1 - i]] = jnp.zeros((DH, DH), BF16)
            for j in range(len(tails)):
                gsb_tail[j, s, SIDES[i], SIDES[1 - i]] = jnp.zeros((DH, DH), BF16)

    class Chain:
        def __init__(self, own, part, arrived, arrived2, out, out2, rel, state, sems, late, flags, place, onward, split):
            self.own, self.part, self.arrived, self.arrived2 = own, part, arrived, arrived2
            self.out, self.out2, self.rel, self.state, self.sems = out, out2, rel, state, sems
            f0, f1 = flags
            self.c_own, self.c_part = jnp.where(late, 1.0, f1), jnp.where(late, f1, 1.0)
            self.c_in = f0 * f1
            self.own_part, self.own_in = jnp.where(late, 1.0, 0.0), jnp.where(late, f0, 1.0)
            self.rel_own, self.rel_in = jnp.where(late, 0.0, 1.0), jnp.where(late, 1.0, f0)
            self.place, self.onward = place, onward
            self.is_first, self.is_last = place == 0, place == seqs - 1
            self.split = sum(1 << p for p in split)

        def remote(self, src, dst, kind, p, where):
            return pltpu.make_async_remote_copy(
                src_ref=src, dst_ref=dst, send_sem=self.sems.at[kind, 0, p], recv_sem=self.sems.at[kind, 1, p],
                device_id=where, device_id_type=MESH,
            )

        def to_partner(self, p):
            return self.remote(self.own.at[2 * p + 1 - core], self.part.at[p], 0, p, other_core)

        def to_next(self, p):
            return self.remote(self.out.at[p], self.arrived.at[p], 1, p, self.onward)

        def relay(self, p):
            return self.remote(self.rel.at[p], self.state.at[2 * p + core], 2, p, other_core)

        def after(self, p):
            return self.remote(self.out2.at[p], self.arrived2.at[p], 3, p, self.onward)

        def keep(self, p, own, part, came):
            self.rel[p] = self.rel_own * own + self.rel_in * came
            self.relay(p).start()
            self.state[2 * p + core] = self.own_part * part + self.own_in * came

        def step(self, p):
            self.to_partner(p).wait_recv()

            @pl.when(jnp.logical_not(self.is_first))
            def _():
                self.to_next(p).wait_recv()

            own, part, came = self.own[2 * p + core], self.part[p], self.arrived[p]

            @pl.when(jnp.logical_not(self.is_last))
            def _():
                self.out[p] = self.c_own * own + self.c_part * part + self.c_in * came
                self.to_next(p).start()

            self.keep(p, own, part, came)

        def early(self, p):
            self.to_partner(p).wait_recv()
            both = self.c_own * self.own[2 * p + core] + self.c_part * self.part[p]

            @pl.when(self.place == 1)
            def _():
                self.out[p] = both

            @pl.when(self.place == 2)
            def _():
                self.to_next(p).wait_recv()
                self.out[p] = both + self.c_in * self.arrived[p]

            self.to_next(p).start()

        def rest(self, p):
            @pl.when(self.is_first | self.is_last)
            def _():
                self.to_partner(p).wait_recv()

            @pl.when((self.place == 1) | self.is_last)
            def _():
                self.to_next(p).wait_recv()

            @pl.when(self.is_first)
            def _():
                self.out[p] = self.c_own * self.own[2 * p + core] + self.c_part * self.part[p]
                self.to_next(p).start()

            @pl.when(self.place == 1)
            def _():
                self.out2[p] = self.c_in * self.arrived[p]
                self.after(p).start()

            @pl.when(self.place == 2)
            def _():
                self.after(p).wait_recv()

            self.keep(p, self.own[2 * p + core], self.part[p], self.arrived[p] + self.arrived2[p])

        def take(self, p):
            self.remote(self.rel.at[p], self.state.at[2 * p + 1 - core], 2, p, other_core).wait_recv()

        def finish(self, p):
            self.to_partner(p).wait_send()
            self.relay(p).wait_send()

            @pl.when(jnp.logical_not(self.is_last))
            def _():
                self.to_next(p).wait_send()

            if self.split:
                other_way = lax.shift_right_logical(jnp.int32(self.split), p) & 1

                @pl.when((self.place == 1) & (other_way == 1))
                def _():
                    self.after(p).wait_send()

    ahead = Chain(
        fown, fpart, fin, fin2, fout, fout2, frel, fstate, fsem, core == 1, flags_f,
        chip, chip_on, split_f,
    )
    back = Chain(
        bown, bpart, bin_, bin2, bout, bout2, brel, bstate, bsem, core == 0, flags_b,
        seqs - 1 - chip, chip_back, split_b,
    )

    def local(p):
        load(0, k_hbm, ks, p).wait()
        load(1, v_hbm, vs, p).wait()
        sums = [tn(ks[p, s] * tail_m[s], vs[p, s]) for s in HALVES]
        for i, side in enumerate(SIDES):
            up, low = (x[side, side] for x in sums)
            fhalf[2 * p + i] = up
            fown[2 * p + i] = low + up_last * up

    def scores(p):
        load(2, q_hbm, qs, p).wait()
        raw = [nt(qs[p, HALVES[s], SIDES[i]], ks[p, HALVES[s], SIDES[i]]) for s, i in PLACES]
        kept = [(x * mask[s]).astype(BF16) for x, (s, i) in zip(raw, PLACES)]
        sums = [nn(w, vs[p, HALVES[s], SIDES[i]]) for w, (s, i) in zip(kept, PLACES)]
        for w, x, (s, i) in zip(kept, sums, PLACES):
            ws[p, s, i] = w
            acc[p, HALVES[s], SIDES[i]] = x

    def forward(p):
        ahead.take(p)
        load(3, d_hbm, ds, p).wait()
        for i, side in enumerate(SIDES):
            state = fstate[2 * p + i]
            sb[p, 0, side, side] = (state * (1.0 / DH)).astype(BF16)
            sb[p, 1, side, side] = ((up_before * state + fhalf[2 * p + i]) * (1.0 / DH)).astype(BF16)
        carried = [nn(qs[p, HALVES[s]] * fwd_m[HALVES[s]], sb[p, s]) for s in range(2)]
        gains = [gain[pl.ds(2 * p + i, 1), :] for i in range(2)]
        made = []
        for s, i in PLACES:
            half, side = HALVES[s], SIDES[i]
            attn = acc[p, half, side] + carried[s][:, side]
            inverse = lax.rsqrt(jnp.mean(attn * attn, axis=-1, keepdims=True) + 1e-5)
            normed = attn * inverse
            mixed = (normed * gains[i]).astype(BF16)
            d = ds[p, half, side].astype(F32)
            terms = jnp.sum(d * normed, axis=0, keepdims=True)
            g = d * gains[i]
            inner = jnp.mean(g * normed, axis=-1, keepdims=True)
            made.append((mixed, (inverse * (g - normed * inner)).astype(BF16), terms))
        for (s, i), (mixed, grad, terms) in zip(PLACES, made):
            mix[HALVES[s], pl.ds(pl.multiple_of(p * PAIR + i * DH, DH), DH)] = mixed
            gs[p, HALVES[s], SIDES[i]] = grad
        for i, side in enumerate(SIDES):
            gslots[rank, pl.ds(2 * p + i, 1), :] = made[i][2] + made[2 + i][2]
        sums = [tn(qs[p, s] * head_m[s], gs[p, s]) for s in HALVES]
        for i, side in enumerate(SIDES):
            up, low = (x[side, side] for x in sums)
            bhalf[2 * p + i] = low
            bown[2 * p + i] = up + down_first * low
        back.to_partner(p).start()

    def later_state(p, low):
        back.take(p)
        for i, side in enumerate(SIDES):
            state = bstate[2 * p + i]
            low[1, side, side] = (state * (1.0 / DH)).astype(BF16)
            low[0, side, side] = ((down_after * state + bhalf[2 * p + i]) * (1.0 / DH)).astype(BF16)

    def grads(p):
        later_state(p, gsb)
        made = input_grads(p, qs, ks, vs, gs, ws, sb, gsb, mask, fwd_m, bwd_m)
        for (s, i), values in zip(PLACES, made):
            for ref, value in zip((gq, gk, gv), values):
                ref[HALVES[s], pair_columns(p, i, DH)] = value

    def gcopy(o):
        return pltpu.make_async_remote_copy(
            src_ref=gslots.at[rank], dst_ref=gslots.at[rank], send_sem=gsend.at[o], recv_sem=grecv.at[rank],
            device_id=device(lax.rem(rank + o, n)), device_id_type=MESH,
        )

    def share_gain(p):
        for o in range(1, n):
            gcopy(o).start()

    orders = [[(u, p) for u, p in order if u != "D" or p not in late] for order, late in zip(orders, tail_lists(seqs, pairs))]
    steps = max(len(order) for order in orders)
    words = []
    for at in range(0, steps, SLOTS):
        word = jnp.int32(0)
        for c, order in enumerate(orders):
            codes = [UNITS.index(u) + (p << 4) for u, p in order[at:at + SLOTS]]
            codes += [15] * (SLOTS - len(codes))
            bits = sum(code << (7 * j) for j, code in enumerate(codes))
            word = jnp.where(chip == c, jnp.int32(bits), word)
        words.append(word)
    held = min(4, pairs)

    def unit_at(i):
        group = lax.div(i, SLOTS)
        word = words[0]
        for g in range(1, len(words)):
            word = jnp.where(group == g, words[g], word)
        code = lax.shift_right_logical(word, 7 * lax.rem(i, SLOTS)) & 127
        return code & 15, lax.shift_right_logical(code, 4)

    def local_and_send(i, p):
        local(p)

        @pl.when(i == held - 1)
        def _():
            inner = (chip > 0) & (chip < seqs - 1)

            @pl.when(inner)
            def _():
                pl.semaphore_wait(barrier, 3)

            @pl.when(jnp.logical_not(inner))
            def _():
                pl.semaphore_wait(barrier, 2)

            for j in range(held):
                ahead.to_partner(unit_at(j)[1]).start()

        @pl.when(i >= held)
        def _():
            ahead.to_partner(p).start()

    def one(fn):
        return lambda i, p: fn(p)

    work = (local_and_send,) + tuple(
        one(fn) for fn in (
            scores, ahead.step, forward, back.step, grads, share_gain, ahead.early, ahead.rest, back.early, back.rest,
        )
    )
    if not split_f + split_b:
        work = work[:7]

    def step(i, c):
        unit, p = unit_at(i)
        for u, fn in enumerate(work):
            pl.when(unit == u)(functools.partial(fn, i, p))
        return c

    lax.fori_loop(0, steps, step, 0)
    for j, p in enumerate(tails):
        later_state(p, gsb_tail.at[j])

    for o in range(1, n):
        src = lax.rem(rank + n - o, n)
        pltpu.make_async_remote_copy(
            src_ref=gslots.at[src], dst_ref=gslots.at[src], send_sem=gsend.at[o], recv_sem=grecv.at[src],
            device_id=device(src), device_id_type=MESH,
        ).wait_recv()
        gcopy(o).wait_send()
    summed = gslots[0]
    for i in range(1, n):
        summed = summed + gslots[i]
    ggain[...] = summed * (1.0 / math.sqrt(total))

    def finish(p):
        ahead.finish(p)
        back.finish(p)

    each(finish)


def writer(
    pairs, seqs,
    mix, gq, gk, gv, ggain, qs, ks, vs, gs, ws, sb, gsb_tail, mask, fwd_m, bwd_m,
    mix_hbm, gq_hbm, gk_hbm, gv_hbm, ggain_hbm,
    made, sems, tail_sems, whole_sems,
):
    outs = tuple(zip((gq, gk, gv), (gq_hbm, gk_hbm, gv_hbm)))
    tails = tails_of(seqs, pairs, lax.axis_index("seq"))
    whole = [
        pltpu.make_async_copy(mix, mix_hbm, whole_sems.at[0]), pltpu.make_async_copy(ggain, ggain_hbm, whole_sems.at[1])
    ]
    for copy in whole:
        copy.start()

    def copies(p):
        here = pair_columns(p)
        return [
            pltpu.make_async_copy(ref.at[:, here], hbm.at[:, here], sems.at[i, p]) for i, (ref, hbm) in enumerate(outs)
        ]

    def ready(p, act):
        @pl.when(functools.reduce(jnp.logical_and, [p != tail for tail in tails]))
        def _():
            for copy in copies(p):
                act(copy)

    for p in range(pairs):
        ready(p, lambda copy: copy.start())
    tail_copies = []
    for j, p in enumerate(tails):
        found = input_grads(p, qs, ks, vs, gs, ws, sb, gsb_tail.at[j], mask, fwd_m, bwd_m)
        for (s, i), values in zip(PLACES, found):
            for o, value in enumerate(values):
                made[j, o, HALVES[s], SIDES[i]] = value
        for o, (ref, hbm) in enumerate(outs):
            tail_copies.append(pltpu.make_async_copy(made.at[j, o], hbm.at[:, pair_columns(p)], tail_sems.at[j, o]))
            tail_copies[-1].start()
    for copy in whole + tail_copies:
        copy.wait()
    for p in range(pairs):
        ready(p, lambda copy: copy.wait())


def shards(queries, keys, values, d_out, doc_lengths, gain):
    tokens, width = queries.shape
    pairs = width // PAIR
    heads = 2 * pairs
    seqs, reps = lax.axis_size("seq"), lax.axis_size("rep")
    n = seqs * reps
    slab = pltpu.VMEM((pairs, tokens, PAIR), BF16)
    rows = pltpu.VMEM((tokens, PAIR), BF16)
    state = pltpu.VMEM((heads, DH, DH), F32)
    half = pltpu.VMEM((pairs, DH, DH), F32)
    dma = pltpu.SemaphoreType.DMA
    big = jax.ShapeDtypeStruct((tokens, width), BF16)
    hbm = pl.BlockSpec(memory_space=pltpu.HBM)
    in_hbm = functools.partial(pltpu.with_memory_space_constraint, memory_space=pltpu.HBM)
    vmem = pl.BlockSpec(memory_space=pltpu.VMEM)
    shapes = (big, big, big, big, jax.ShapeDtypeStruct((heads, DH), F32))
    tails = min(TAIL, pairs)

    def array(*shape, dtype=BF16):
        return jax.ShapeDtypeStruct(shape, dtype)

    pair_rows = array(pairs, tokens, PAIR)
    held = (
        pair_rows, pair_rows, pair_rows, pair_rows,
        array(pairs, 2, 2, HALF, HALF), array(pairs, 2, PAIR, PAIR), array(tails, 2, PAIR, PAIR),
        array(2, HALF, HALF, dtype=F32), array(tokens, PAIR), array(tokens, PAIR),
    )
    made = pl.pallas_call(
        functools.partial(kernel, pairs, tokens, seqs, reps, doc_lengths.shape[0]),
        out_shape=shapes + held,
        in_specs=[hbm] * 6,
        out_specs=(vmem,) * (len(shapes) + len(held)),
        scratch_shapes=[
            pltpu.SMEM(doc_lengths.shape, jnp.int32),
            pltpu.VMEM((heads, DH), F32),
            slab,
            pltpu.VMEM((pairs, tokens, PAIR), F32),
            rows, rows,
            state, state, half, half, half, half, half, half, state,
            state, state, half, half, half, half, half, half, state,
            pltpu.VMEM((2, PAIR, PAIR), BF16),
            pltpu.VMEM((n, heads, DH), F32),
            dma((4, pairs)), dma((2,)), dma((4, 2, pairs)), dma((4, 2, pairs)),
            dma((n,)), dma((n,)),
        ],
        compiler_params=pltpu.CompilerParams(
            collective_id=0, has_side_effects=True, vmem_limit_bytes=26 << 20
        ),
    )(*(in_hbm(x) for x in (doc_lengths, gain.reshape(heads, DH), queries, keys, values, d_out)))
    out = pl.pallas_call(
        functools.partial(writer, pairs, seqs),
        out_shape=shapes,
        in_specs=[vmem] * len(made),
        out_specs=(hbm,) * len(shapes),
        scratch_shapes=[
            pltpu.VMEM((tails, 3, tokens, PAIR), BF16), dma((3, pairs)), dma((tails, 3)), dma((2,)),
        ],
        compiler_params=pltpu.CompilerParams(vmem_limit_bytes=8 << 20),
    )(*made)
    return (*out[:4], out[4].reshape(1, width))


def solution(mesh):
    token = P(("groups", "seq", "rep"), "head")
    return jax.shard_map(
        shards,
        mesh=mesh,
        in_specs=(token, token, token, token, P("groups"), P("head")),
        out_specs=(token, token, token, token, P("groups", "head")),
        check_vma=False,
    )
```
